128 devices in a mesh: wide: 32 (over z, x, core), narrow: 4 (over y).
Axes of the slice: x: 4, y: 4, z: 4, core: 2. Of those that a mesh axis runs over, the one named last changes fastest.
Arguments:
- fields: bfloat16 [24, 128, 32, 512], P(None, None, 'wide', 'narrow'), may hold values from -6 to 6
- neighbors: int32 [4, 32, 512], P(None, 'wide', 'narrow'), may hold values from 0 to 511, as said below
- cost: int32 [32, 512], P('wide', 'narrow'), may hold values from 1 to 8
- dest: int32 [32, 512], P('wide', 'narrow'), may hold values from 0 to 127, as said below
- diffusivity: bfloat16 [128, 32, 512], P(None, 'wide', 'narrow'), may hold values from 0.099609375 to 1
- operators: bfloat16 [8, 128, 128], replicated
Outputs:
- new_fields: bfloat16 [24, 128, 32, 512], P(None, None, 'wide', 'narrow')
- column_burden: float32 [128, 24, 128], P(('wide', 'narrow'))
The draws below stay inside these ranges and needn't reach their ends.
Inputs may be any that keep to these rules, and one draw needn't show every extreme that they name: neighbors[k, r, c] lies within 2 columns of c along the row, counted cyclically over 512, and is never c. `dest`: stretch w * (narrow devices) + n is the device at index w of wide and n of narrow. Of the columns of one device, at most 2 go to one stretch, and exactly 2 go to some stretches; every stretch receives exactly 128 columns in all. Each device deals its columns, in order of rising cost, to its stretches in turn, so that the stretches' summed costs are nearly even while the grid blocks' are not.
All inputs are finite; a program needn't handle non-finite values.
Results may differ from the reference program's by a relative error of at most 0.0068.
Values may be sent and summed in bfloat16 or wider, within the bound.
No kernel may reach another device: no remote copies, remote signals or barrier semaphores. Data moves between devices by JAX's collectives and lax.ppermute only.
A program may use at most 64 MiB of HBM per device.

```python
import math
import jax
import jax.numpy as jnp
import numpy as np
from jax import lax

LEVELS = 128
TRACERS = 24
RD = 1
CD = 128
REACH = 2
NEIGH = 4
KMAX = 8
STRETCHES = 128
NCD = 128
CAP = 2
NR = 32
NC = 512


def to_grid(values):
    wide_n = NR // RD
    narrow_n = NC // CD
    return values.reshape(wide_n, narrow_n, RD, CD).transpose(0, 2, 1, 3).reshape(NR, NC).astype(jnp.int32)


def plan_columns(key):
    base = jax.random.fold_in(key, 11)
    key_ceil, key_cost, key_pos, key_shift, key_tie = jax.random.split(base, 5)
    ceilings = 1 + jax.random.permutation(key_ceil, STRETCHES) % KMAX
    costs = jax.random.randint(key_cost, (STRETCHES, NCD), 1, ceilings[:, None] + 1)
    picked = jax.random.randint(key_pos, (STRETCHES, 1), 0, NCD)
    place = jnp.arange(NCD, dtype=jnp.int32)[None, :]
    costs = jnp.where(place == picked, ceilings[:, None], costs)
    tie_keys = jax.random.split(key_tie, STRETCHES)
    ties = jax.vmap(lambda one_key: jax.random.permutation(one_key, NCD))(tie_keys)
    order = jnp.argsort(costs * NCD + ties, axis=1)
    key_rank, key_mix = jax.random.split(key_shift)
    values_all = jnp.arange(STRETCHES, dtype=jnp.int32)
    special = (values_all == 1) | (values_all == STRETCHES - 1) | (values_all == STRETCHES // 2)
    ranks = jax.random.permutation(key_rank, STRETCHES).astype(jnp.int32)
    score = ranks + STRETCHES * (1 - special.astype(jnp.int32))
    chosen = jnp.argsort(score)[:3 * STRETCHES // 4].astype(jnp.int32)
    shifts = chosen[jax.random.permutation(key_mix, 3 * STRETCHES // 4)]
    counts = [CAP] * (STRETCHES // 4) + [CAP // 2] * (STRETCHES // 2)
    sequence = []
    for round_index in range(CAP):
        for shift_index in range(len(counts)):
            if counts[shift_index] > round_index:
                sequence.append(shift_index)
    per_rank = shifts[np.array(sequence, dtype=np.int32)]
    sources = jnp.arange(STRETCHES, dtype=jnp.int32)[:, None]
    values = (sources + per_rank[None, :]) % STRETCHES
    placed = jax.vmap(lambda one_order, one_value: jnp.zeros((NCD,), jnp.int32).at[one_order].set(one_value))(order, values)
    return (costs, placed)


def draw_neighbors(key, part):
    picked = jax.random.randint(key, (NEIGH, NR, NC), 0, 2 * REACH)
    offset = picked - REACH
    offset = offset + (offset >= 0).astype(jnp.int32)
    column = jnp.arange(NC, dtype=jnp.int32)[None, None, :]
    return ((column + offset) % NC).astype(jnp.int32)


def draw_cost(key, part):
    costs, placed = plan_columns(key)
    return to_grid(costs)


def draw_dest(key, part):
    costs, placed = plan_columns(key)
    return to_grid(placed)


def draw_operators(key, part):
    key_diag, key_off = jax.random.split(jax.random.fold_in(key, 23))
    diagonal = jax.random.uniform(key_diag, (KMAX, LEVELS), jnp.float32, 0.4, 0.9)
    offdiag = jax.random.normal(key_off, (KMAX, LEVELS, LEVELS), jnp.float32) * (0.3 / math.sqrt(LEVELS))
    identity = jnp.eye(LEVELS, dtype=jnp.float32)
    return (offdiag * (1.0 - identity) + diagonal[..., :, None] * identity).astype(jnp.bfloat16)


def steps_of(rng, dims, cuts, smallest, top_value):
    loudness = 1.0
    for dim, parts in cuts:
        heights = jax.random.uniform(jax.random.fold_in(jax.random.fold_in(rng, 6), dim), (parts,), jnp.float32, smallest / len(cuts), top_value / len(cuts))
        loudness = loudness * jnp.repeat(jnp.exp(heights), dims[dim] // parts).reshape((-1,) + (1,) * (len(dims) - 1 - dim))
    return loudness


def gaussian(rng, shape, scale, most, shards=(), kind=jnp.bfloat16):
    loudness = steps_of(rng, shape, shards, -0.22, 0.18) if shards else 1.0
    drawn = jax.random.normal(rng, shape, jnp.float32) * scale * loudness
    return jnp.minimum(jnp.maximum(drawn, -most), most).astype(kind)


def setup_inputs(seed: int = 0) -> dict:
    streams_of = jax.random.split(jax.random.key(seed), 7)
    fields = gaussian(streams_of[0], (TRACERS, LEVELS, NR, NC), 1.0, 6.0, ((2, 32), (3, 4)))
    neighbors = draw_neighbors(jax.random.fold_in(streams_of[6], 71), 0)
    cost = draw_cost(jax.random.fold_in(streams_of[6], 71), 0)
    dest = draw_dest(jax.random.fold_in(streams_of[6], 71), 0)
    diffusivity = jnp.clip(jnp.exp(math.log(1.0) - 2.306499 * jax.random.uniform(streams_of[4], (LEVELS, NR, NC), jnp.float32) ** steps_of(streams_of[4], (LEVELS, NR, NC), ((1, 32), (2, 4)), -0.2, 0.2)), 0.099609375, 1.0).astype(jnp.bfloat16)
    operators = draw_operators(jax.random.fold_in(streams_of[6], 71), 0)
    return dict(fields=fields, neighbors=neighbors, cost=cost, dest=dest, diffusivity=diffusivity, operators=operators)


mixing_rate = 0.2


def level_laplace(values, axis):
    length = values.shape[axis]
    first = lax.slice_in_dim(values, 0, 1, axis=axis)
    final = lax.slice_in_dim(values, length - 1, length, axis=axis)
    above = jnp.concatenate([first, lax.slice_in_dim(values, 0, length - 1, axis=axis)], axis=axis)
    below = jnp.concatenate([lax.slice_in_dim(values, 1, length, axis=axis), final], axis=axis)
    return above + below - 2.0 * values


def reference(fields, neighbors, cost, dest, diffusivity, operators):
    tracer_n, level_n, row_n, col_n = fields.shape
    column = jnp.arange(col_n, dtype=jnp.int32)
    offset = (neighbors - column[None, None, :] + REACH) % col_n - REACH
    shift_list = [shift_by for shift_by in range(-REACH, REACH + 1) if shift_by != 0]
    weights = [jnp.sum((offset == shift_by).astype(jnp.float32), axis=0) for shift_by in shift_list]

    def dynamics(tracer):
        values = tracer.astype(jnp.float32)
        summed = (1.0 - NEIGH * mixing_rate) * values
        for shift_by, weight in zip(shift_list, weights):
            summed = summed + mixing_rate * weight * jnp.roll(values, -shift_by, axis=2)
        return summed.astype(jnp.bfloat16)

    dyn = lax.map(dynamics, fields)
    total = row_n * col_n
    dyn_flat = dyn.reshape(tracer_n, level_n, total)
    dyn_cols = jnp.moveaxis(dyn_flat, 2, 0)
    coef_cols = diffusivity.reshape(level_n, total).T
    ops = operators.astype(jnp.float32)
    steps_flat = cost.reshape(-1).astype(jnp.float32)
    row_ids = jnp.arange(row_n, dtype=jnp.int32)[:, None]
    col_ids = jnp.arange(col_n, dtype=jnp.int32)[None, :]
    source = (row_ids // RD) * (col_n // CD) + col_ids // CD
    place = (row_ids % RD) * CD + col_ids % CD
    sort_key = dest * total + source * (RD * CD) + place
    order = jnp.argsort(sort_key.reshape(-1)).astype(jnp.int32)
    groups = order.reshape(STRETCHES, -1)

    def stretch_physics(members):
        start = jnp.take(dyn_cols, members, axis=0)
        coefs = jnp.take(coef_cols, members, axis=0).astype(jnp.float32)[:, None, :]
        steps = jnp.take(steps_flat, members)[:, None, None]
        gains = steps / (4.0 * KMAX) * coefs
        start_f = start.astype(jnp.float32)
        current = start
        final = jnp.zeros_like(start_f)
        for step_index in range(KMAX):
            mixed = jnp.einsum("lm,cqm->cql", ops[step_index], current.astype(jnp.float32))
            widened = mixed + gains * level_laplace(mixed, 2)
            count = float(step_index + 1)
            final = jnp.where(steps == count, widened, final)
            current = jnp.where(steps >= count, widened.astype(jnp.bfloat16), current)
        change = final - start_f
        return change.astype(jnp.bfloat16), jnp.sum(change, axis=2).T

    tends, burdens = lax.map(stretch_physics, groups)
    tend_cols = jnp.zeros((total, tracer_n, level_n), jnp.bfloat16).at[order].set(
        tends.reshape(total, tracer_n, level_n))
    tend_all = jnp.moveaxis(tend_cols, 0, 2)

    def combine(pair):
        return (pair[0].astype(jnp.float32) + pair[1].astype(jnp.float32)).astype(jnp.bfloat16)

    result = lax.map(combine, (dyn_flat, tend_all))
    return result.reshape(fields.shape), burdens
```

```python
import functools

import jax
import jax.numpy as jnp
from jax import lax
from jax.experimental import pallas as pl
from jax.experimental.pallas import tpu as pltpu
from jax.sharding import PartitionSpec as P

REACH = 2
NEIGH = 4
KMAX = 8
MIX = 0.2
TRACERS = 24
LEVELS = 128
COLS = 128
GROUP = 4
SLOT = 32

F32 = jnp.float32
BF16 = jnp.bfloat16
NT = (((1,), (1,)), ((), ()))


def iota(shape, dim):
    return lax.broadcasted_iota(jnp.int32, shape, dim)


def dot(a, b):
    return jnp.dot(a, b, preferred_element_type=F32)


def split(x):
    high = x.astype(BF16)
    return high, (x - high.astype(F32)).astype(BF16)


def level_laplace(z):
    above = jnp.concatenate([z[:1], z[:-1]], axis=0)
    below = jnp.concatenate([z[1:], z[-1:]], axis=0)
    return above + below - 2.0 * z


def main_kernel(
    fields, before, after, neighbors, cost, dest, coef, operators,
    out, sent, ops, near, far, halo, dyn, burden,
):
    for s in range(KMAX):
        op = operators[s]
        ops[s, :LEVELS] = op
        ops[s, LEVELS:] = level_laplace(op.astype(F32)).astype(BF16)

    place = iota((COLS, COLS), 0)
    here = iota((COLS, COLS), 1)
    lane = iota((1, COLS), 1)
    weight = (place == here).astype(F32)
    edge = jnp.zeros((COLS, COLS), F32)
    tag = place // TRACERS
    tag = jnp.where(tag < REACH, tag - REACH, tag + (COLS - REACH))
    for k in range(NEIGH):
        offset = ((neighbors[k : k + 1, :] - lane + REACH) & (COLS - 1)) - REACH
        reads = lane + offset
        weight += (place == reads).astype(F32)
        edge += (tag == reads).astype(F32)
    near[...] = weight.astype(BF16)
    far[...] = edge
    owner = place - (place // TRACERS) * TRACERS
    rows = jnp.concatenate(
        [before[0], before[1], after[0], after[1], jnp.zeros((SLOT, LEVELS), BF16)], axis=0
    )
    halo[...] = rows.astype(F32).T.astype(BF16)

    count = cost[...]
    scale = coef[...].astype(F32) * (count.astype(F32) / (4.0 * KMAX))
    scale2 = jnp.concatenate([scale, scale], axis=1)
    count2 = jnp.concatenate([count, count], axis=1)
    burden[...] = jnp.zeros((SLOT, COLS), F32)

    def dynamics(q, carry):
        mine = jnp.where(owner == q, far[...], 0.0).astype(BF16)
        both = jnp.concatenate([fields[q], halo[...]], axis=1)
        summed = dot(both, jnp.concatenate([near[...], mine], axis=0))
        dyn[q] = (MIX * summed).astype(BF16)
        return carry

    lax.fori_loop(0, TRACERS, dynamics, 0, unroll=4)

    pairs = GROUP // 2

    def group(g, carry):
        base = g * GROUP
        first = [
            jnp.concatenate([dyn[base + 2 * p], dyn[base + 2 * p + 1]], axis=1) for p in range(pairs)
        ]
        state = list(first)
        final = [None] * pairs
        for s in range(KMAX):
            for p in range(pairs):
                both = dot(ops[s], state[p])
                widened = both[:LEVELS] + scale2 * both[LEVELS:]
                final[p] = widened if s == 0 else jnp.where(count2 > s, widened, final[p])
                state[p] = widened.astype(BF16)
        for p in range(pairs):
            start = first[p].astype(F32)
            change = final[p] - start
            total = jnp.sum(change, axis=0, keepdims=True)
            result = (start + change.astype(BF16).astype(F32)).astype(BF16)
            for i in range(2):
                q = base + 2 * p + i
                out[q] = result[:, i * COLS : (i + 1) * COLS]
                burden[pl.ds(q, 1), :] = total[:, i * COLS : (i + 1) * COLS]
        return carry

    lax.fori_loop(0, TRACERS // GROUP, group, 0)

    target = jnp.broadcast_to(dest[...], (COLS, COLS))
    same = (target.astype(F32).T == target.astype(F32)) & (place < here)
    turn = jnp.sum(same.astype(F32), axis=0, keepdims=True)
    to = (target == place).astype(F32)
    picked = jnp.concatenate([to * (turn == 0.0), to * (turn == 1.0)], axis=1).astype(BF16)
    values = burden[...] + (iota((SLOT, COLS), 0) == TRACERS).astype(F32)
    none = jnp.zeros((SLOT, COLS), BF16)
    total = jnp.zeros((COLS, COLS), F32)
    for part in split(values):
        wide = jnp.concatenate(
            [
                jnp.concatenate([part, none], axis=1),
                jnp.concatenate([none, part], axis=1),
                jnp.zeros((2 * SLOT, 2 * COLS), BF16),
            ],
            axis=0,
        )
        total += lax.dot_general(picked, wide, NT, preferred_element_type=F32)
    sent[...] = total


def order_kernel(received, out):
    values = received[...]
    place = iota((COLS, COLS), 0)
    here = iota((COLS, COLS), 1)
    flags = values.astype(BF16)
    earlier = dot((here < place).astype(BF16), flags)
    first = values[:, TRACERS : TRACERS + 1]
    second = values[:, SLOT + TRACERS : SLOT + TRACERS + 1]
    rank = earlier[:, TRACERS : TRACERS + 1] + earlier[:, SLOT + TRACERS : SLOT + TRACERS + 1]
    spot = here.astype(F32)
    chosen = jnp.concatenate(
        [
            jnp.where(spot == rank, first, 0.0),
            jnp.where(spot == rank + first, second, 0.0),
        ],
        axis=0,
    ).astype(BF16)
    turned = values.T
    rows = jnp.concatenate([turned[:SLOT], turned[SLOT : 2 * SLOT]], axis=1)
    high, low = split(rows)
    out[...] = (dot(high, chosen) + dot(low, chosen))[:TRACERS]


def local(fields, neighbors, cost, dest, diffusivity, operators):
    size = lax.axis_size("narrow")
    up = [(i, (i + 1) % size) for i in range(size)]
    down = [(j, i) for i, j in up]
    flat = fields.reshape(TRACERS, LEVELS, COLS)
    before = lax.ppermute(flat[:, :, COLS - REACH :].transpose(2, 0, 1), "narrow", up)
    after = lax.ppermute(flat[:, :, :REACH].transpose(2, 0, 1), "narrow", down)
    new, sent = pl.pallas_call(
        main_kernel,
        out_shape=(
            jax.ShapeDtypeStruct((TRACERS, LEVELS, COLS), BF16),
            jax.ShapeDtypeStruct((COLS, COLS), F32),
        ),
        in_specs=[pl.BlockSpec(memory_space=pltpu.VMEM)] * 8,
        out_specs=[pl.BlockSpec(memory_space=pltpu.VMEM)] * 2,
        scratch_shapes=[
            pltpu.VMEM((KMAX, 2 * LEVELS, LEVELS), BF16),
            pltpu.VMEM((COLS, COLS), BF16),
            pltpu.VMEM((COLS, COLS), F32),
            pltpu.VMEM((LEVELS, COLS), BF16),
            pltpu.VMEM((TRACERS, LEVELS, COLS), BF16),
            pltpu.VMEM((SLOT, COLS), F32),
        ],
        name="physics",
    )(
        flat, before, after, neighbors.reshape(NEIGH, COLS), cost, dest,
        diffusivity.reshape(LEVELS, COLS), operators,
    )
    received = lax.all_to_all(sent, ("wide", "narrow"), split_axis=0, concat_axis=0, tiled=True)
    burden = pl.pallas_call(
        order_kernel,
        out_shape=jax.ShapeDtypeStruct((TRACERS, COLS), F32),
        in_specs=[pl.BlockSpec(memory_space=pltpu.VMEM)],
        out_specs=pl.BlockSpec(memory_space=pltpu.VMEM),
        name="order",
    )(received)
    return new.reshape(fields.shape), burden[None]


def solution(mesh):
    in_specs = (
        P(None, None, "wide", "narrow"),
        P(None, "wide", "narrow"),
        P("wide", "narrow"),
        P("wide", "narrow"),
        P(None, "wide", "narrow"),
        P(),
    )
    out_specs = (P(None, None, "wide", "narrow"), P(("wide", "narrow"), None, None))
    return jax.shard_map(local, mesh=mesh, in_specs=in_specs, out_specs=out_specs, check_vma=False)
```

```python
import functools

import jax
import jax.numpy as jnp
from jax import lax
from jax.experimental import pallas as pl
from jax.experimental.pallas import tpu as pltpu
from jax.sharding import PartitionSpec as P

REACH = 2
NEIGH = 4
KMAX = 8
MIX = 0.2
TRACERS = 24
LEVELS = 128
COLS = 128
GROUP = 8
SLOT = 32
ROOM = 24 << 20

F32 = jnp.float32
BF16 = jnp.bfloat16
NT = (((1,), (1,)), ((), ()))


def iota(shape, dim):
    return lax.broadcasted_iota(jnp.int32, shape, dim)


def dot(a, b):
    return jnp.dot(a, b, preferred_element_type=F32)


def split(x):
    high = x.astype(BF16)
    return high, (x - high.astype(F32)).astype(BF16)


def level_laplace(z):
    above = jnp.concatenate([z[:1], z[:-1]], axis=0)
    below = jnp.concatenate([z[1:], z[-1:]], axis=0)
    return above + below - 2.0 * z


def edge_kernel(fields, left, right, rows):
    place = iota((8, COLS), 0)
    lane = iota((8, COLS), 1)
    edge = jnp.where(place < REACH, place, place + (COLS - 2 * REACH))
    pick = (lane == edge).astype(BF16)
    for q in range(TRACERS):
        got = lax.dot_general(pick, fields[q], NT, preferred_element_type=F32)
        for j in range(2 * REACH):
            rows[j * TRACERS + q : j * TRACERS + q + 1, :] = got[j : j + 1]
    left[...] = rows[: REACH * TRACERS].astype(BF16)
    right[...] = rows[REACH * TRACERS :].astype(BF16)


def main_kernel(
    fields, before, after, neighbors, cost, dest, coef, operators,
    out, sent, ops, near, far, halo, dyn, burden,
):
    for s in range(KMAX):
        op = operators[s]
        ops[s, :LEVELS] = op
        ops[s, LEVELS:] = level_laplace(op.astype(F32)).astype(BF16)

    place = iota((COLS, COLS), 0)
    here = iota((COLS, COLS), 1)
    lane = iota((1, COLS), 1)
    weight = (place == here).astype(F32)
    edge = jnp.zeros((COLS, COLS), F32)
    tag = place // TRACERS
    tag = jnp.where(tag < REACH, tag - REACH, tag + (COLS - REACH))
    for k in range(NEIGH):
        offset = ((neighbors[k : k + 1, :] - lane + REACH) & (COLS - 1)) - REACH
        reads = lane + offset
        weight += (place == reads).astype(F32)
        edge += (tag == reads).astype(F32)
    near[...] = weight.astype(BF16)
    far[...] = edge
    owner = place - (place // TRACERS) * TRACERS
    rows = jnp.concatenate(
        [before[...], after[...], jnp.zeros((SLOT, LEVELS), BF16)], axis=0
    )
    halo[...] = rows.astype(F32).T.astype(BF16)

    count = cost[...]
    scale = coef[...].astype(F32) * (count.astype(F32) / (4.0 * KMAX))
    scale2 = jnp.concatenate([scale, scale], axis=1)
    count2 = jnp.concatenate([count, count], axis=1).astype(F32).astype(BF16)
    burden[...] = jnp.zeros((SLOT, COLS), F32)

    for q in range(TRACERS):
        mine = jnp.where(owner == q, far[...], 0.0).astype(BF16)
        both = jnp.concatenate([fields[q], halo[...]], axis=1)
        summed = dot(both, jnp.concatenate([near[...], mine], axis=0))
        dyn[q] = (MIX * summed).astype(BF16)

    pairs = GROUP // 2

    def group(g, carry):
        base = g * GROUP
        state = [
            jnp.concatenate([dyn[base + 2 * p], dyn[base + 2 * p + 1]], axis=1) for p in range(pairs)
        ]
        for s in range(KMAX):
            for p in range(pairs):
                both = dot(ops[s], state[p])
                widened = (both[:LEVELS] + scale2 * both[LEVELS:]).astype(BF16)
                state[p] = widened if s == 0 else jnp.where(count2 > s, widened, state[p])
        for p in range(pairs):
            start = jnp.concatenate([dyn[base + 2 * p], dyn[base + 2 * p + 1]], axis=1).astype(F32)
            change = state[p].astype(F32) - start
            total = jnp.sum(change, axis=0, keepdims=True)
            result = (start + change.astype(BF16).astype(F32)).astype(BF16)
            for i in range(2):
                q = base + 2 * p + i
                out[q] = result[:, i * COLS : (i + 1) * COLS]
                burden[pl.ds(q, 1), :] = total[:, i * COLS : (i + 1) * COLS]
        return carry

    lax.fori_loop(0, TRACERS // GROUP, group, 0)

    target = jnp.broadcast_to(dest[...], (COLS, COLS))
    same = (target.astype(F32).T == target.astype(F32)) & (place < here)
    turn = jnp.sum(same.astype(F32), axis=0, keepdims=True)
    to = (target == place).astype(F32)
    picked = jnp.concatenate([to * (turn == 0.0), to * (turn == 1.0)], axis=1).astype(BF16)
    values = burden[...] + (iota((SLOT, COLS), 0) == TRACERS).astype(F32)
    none = jnp.zeros((SLOT, COLS), BF16)
    total = jnp.zeros((COLS, COLS), F32)
    for part in split(values):
        wide = jnp.concatenate(
            [
                jnp.concatenate([part, none], axis=1),
                jnp.concatenate([none, part], axis=1),
                jnp.zeros((2 * SLOT, 2 * COLS), BF16),
            ],
            axis=0,
        )
        total += lax.dot_general(picked, wide, NT, preferred_element_type=F32)
    sent[...] = total


def order_kernel(received, out):
    values = received[...]
    place = iota((COLS, COLS), 0)
    here = iota((COLS, COLS), 1)
    flags = values.astype(BF16)
    earlier = dot((here < place).astype(BF16), flags)
    first = values[:, TRACERS : TRACERS + 1]
    second = values[:, SLOT + TRACERS : SLOT + TRACERS + 1]
    rank = earlier[:, TRACERS : TRACERS + 1] + earlier[:, SLOT + TRACERS : SLOT + TRACERS + 1]
    spot = here.astype(F32)
    chosen = jnp.concatenate(
        [
            jnp.where(spot == rank, first, 0.0),
            jnp.where(spot == rank + first, second, 0.0),
        ],
        axis=0,
    ).astype(BF16)
    turned = values.T
    rows = jnp.concatenate([turned[:SLOT], turned[SLOT : 2 * SLOT]], axis=1)
    high, low = split(rows)
    out[...] = (dot(high, chosen) + dot(low, chosen))[:TRACERS]


def local(fields, neighbors, cost, dest, diffusivity, operators):
    size = lax.axis_size("narrow")
    up = [(i, (i + 1) % size) for i in range(size)]
    down = [(j, i) for i, j in up]
    flat = fields.reshape(TRACERS, LEVELS, COLS)
    side = jax.ShapeDtypeStruct((REACH * TRACERS, LEVELS), BF16)
    left, right = pl.pallas_call(
        edge_kernel,
        out_shape=(side, side),
        in_specs=[pl.BlockSpec(memory_space=pltpu.VMEM)],
        out_specs=[pl.BlockSpec(memory_space=pltpu.VMEM)] * 2,
        scratch_shapes=[pltpu.VMEM((2 * REACH * TRACERS, LEVELS), F32)],
        compiler_params=pltpu.CompilerParams(vmem_limit_bytes=ROOM),
        name="edge",
    )(flat)
    before = lax.ppermute(right, "narrow", up)
    after = lax.ppermute(left, "narrow", down)
    new, sent = pl.pallas_call(
        main_kernel,
        out_shape=(
            jax.ShapeDtypeStruct((TRACERS, LEVELS, COLS), BF16),
            jax.ShapeDtypeStruct((COLS, COLS), F32),
        ),
        in_specs=[pl.BlockSpec(memory_space=pltpu.VMEM)] * 8,
        out_specs=[pl.BlockSpec(memory_space=pltpu.VMEM)] * 2,
        scratch_shapes=[
            pltpu.VMEM((KMAX, 2 * LEVELS, LEVELS), BF16),
            pltpu.VMEM((COLS, COLS), BF16),
            pltpu.VMEM((COLS, COLS), F32),
            pltpu.VMEM((LEVELS, COLS), BF16),
            pltpu.VMEM((TRACERS, LEVELS, COLS), BF16),
            pltpu.VMEM((SLOT, COLS), F32),
        ],
        compiler_params=pltpu.CompilerParams(vmem_limit_bytes=ROOM),
        name="physics",
    )(
        flat, before, after, neighbors.reshape(NEIGH, COLS), cost, dest,
        diffusivity.reshape(LEVELS, COLS), operators,
    )
    received = lax.all_to_all(sent, ("wide", "narrow"), split_axis=0, concat_axis=0, tiled=True)
    burden = pl.pallas_call(
        order_kernel,
        out_shape=jax.ShapeDtypeStruct((TRACERS, COLS), F32),
        in_specs=[pl.BlockSpec(memory_space=pltpu.VMEM)],
        out_specs=pl.BlockSpec(memory_space=pltpu.VMEM),
        compiler_params=pltpu.CompilerParams(vmem_limit_bytes=ROOM),
        name="order",
    )(received)
    return new.reshape(fields.shape), burden[None]


def solution(mesh):
    in_specs = (
        P(None, None, "wide", "narrow"),
        P(None, "wide", "narrow"),
        P("wide", "narrow"),
        P("wide", "narrow"),
        P(None, "wide", "narrow"),
        P(),
    )
    out_specs = (P(None, None, "wide", "narrow"), P(("wide", "narrow"), None, None))
    return jax.shard_map(local, mesh=mesh, in_specs=in_specs, out_specs=out_specs, check_vma=False)
```

```python
import functools

import jax
import jax.numpy as jnp
from jax import lax
from jax.experimental import pallas as pl
from jax.experimental.pallas import tpu as pltpu
from jax.sharding import PartitionSpec as P

REACH = 2
NEIGH = 4
KMAX = 8
MIX = 0.2
TRACERS = 24
LEVELS = 128
COLS = 128
GROUP = 12
SLOT = 32
TILE = 16
ROOM = 24 << 20

F32 = jnp.float32
BF16 = jnp.bfloat16
NT = (((1,), (1,)), ((), ()))


def iota(shape, dim):
    return lax.broadcasted_iota(jnp.int32, shape, dim)


def dot(a, b):
    return jnp.dot(a, b, preferred_element_type=F32)


def split(x):
    high = x.astype(BF16)
    return high, (x - high.astype(F32)).astype(BF16)


def level_laplace(z):
    above = jnp.concatenate([z[:1], z[:-1]], axis=0)
    below = jnp.concatenate([z[1:], z[-1:]], axis=0)
    return above + below - 2.0 * z


def edge_kernel(fields, left, right, rows):
    place = iota((8, COLS), 0)
    lane = iota((8, COLS), 1)
    edge = jnp.where(place < REACH, place, place + (COLS - 2 * REACH))
    pick = (lane == edge).astype(BF16)
    for q in range(TRACERS):
        got = lax.dot_general(pick, fields[q], NT, preferred_element_type=F32)
        for j in range(2 * REACH):
            rows[j * TRACERS + q : j * TRACERS + q + 1, :] = got[j : j + 1]
    left[...] = rows[: REACH * TRACERS].astype(BF16)
    right[...] = rows[REACH * TRACERS :].astype(BF16)


def plan_kernel(
    neighbors, cost, dest, coef, operators, ops, near, far, scale, pull, picked, pair
):
    for s in range(KMAX):
        op = operators[s]
        lap = level_laplace(op.astype(F32)).astype(BF16)
        pair[s, :LEVELS] = op
        pair[s, LEVELS:] = lap
        for t in range(LEVELS // TILE):
            ops[s, 2 * t * TILE : (2 * t + 1) * TILE] = op[t * TILE : (t + 1) * TILE]
            ops[s, (2 * t + 1) * TILE : (2 * t + 2) * TILE] = lap[t * TILE : (t + 1) * TILE]

    place = iota((COLS, COLS), 0)
    here = iota((COLS, COLS), 1)
    lane = iota((1, COLS), 1)
    weight = (place == here).astype(F32)
    edge = jnp.zeros((COLS, COLS), F32)
    tag = place // TRACERS
    tag = jnp.where(tag < REACH, tag - REACH, tag + (COLS - REACH))
    for k in range(NEIGH):
        offset = ((neighbors[k : k + 1, :] - lane + REACH) & (COLS - 1)) - REACH
        reads = lane + offset
        weight += (place == reads).astype(F32)
        edge += (tag == reads).astype(F32)
    near[...] = weight.astype(BF16)
    far[...] = edge
    steps = jnp.broadcast_to(cost[...].astype(F32), (COLS, COLS))
    scaled = coef[...].astype(F32) * (steps / (4.0 * KMAX))
    scale[...] = scaled

    scaled = scaled.T
    steps = steps.T
    row = jnp.ones((COLS, LEVELS), F32)
    for s in reversed(range(KMAX)):
        parts = []
        for part in zip(split(row), split(scaled * row)):
            parts.append(jnp.concatenate(part, axis=1))
        moved = dot(jnp.concatenate(parts, axis=0), pair[s])
        row = jnp.where(steps > s, moved[:COLS] + moved[COLS:], 1.0)
    pull[...] = (row - 1.0).T

    target = jnp.broadcast_to(dest[...], (COLS, COLS)).astype(F32)
    same = (target.T == target) & (place < here)
    turn = jnp.sum(same.astype(F32), axis=0, keepdims=True)
    to = (target == place.astype(F32)).astype(F32)
    picked[:, :COLS] = (to * (turn == 0.0)).astype(BF16)
    picked[:, COLS:] = (to * (turn == 1.0)).astype(BF16)


def start_kernel(fields, before, after, near, far, pull, picked, dyn, sent, halo, burden):
    rows = jnp.concatenate(
        [before[...], after[...], jnp.zeros((SLOT, LEVELS), BF16)], axis=0
    )
    halo[...] = rows.astype(F32).T.astype(BF16)
    place = iota((COLS, COLS), 0)
    owner = place - (place // TRACERS) * TRACERS
    burden[TRACERS:] = (iota((SLOT - TRACERS, COLS), 0) == 0).astype(F32)

    for q in range(TRACERS):
        mine = jnp.where(owner == q, far[...], 0.0).astype(BF16)
        both = jnp.concatenate([fields[q], halo[...]], axis=1)
        summed = dot(both, jnp.concatenate([near[...], mine], axis=0))
        start = (MIX * summed).astype(BF16)
        dyn[q] = start
        burden[q : q + 1, :] = jnp.sum(pull[...] * start.astype(F32), axis=0, keepdims=True)

    none = jnp.zeros((SLOT, COLS), BF16)
    total = jnp.zeros((COLS, COLS), F32)
    for part in split(burden[...]):
        wide = jnp.concatenate(
            [
                jnp.concatenate([part, none], axis=1),
                jnp.concatenate([none, part], axis=1),
                jnp.zeros((2 * SLOT, 2 * COLS), BF16),
            ],
            axis=0,
        )
        total += lax.dot_general(picked[...], wide, NT, preferred_element_type=F32)
    sent[...] = total


def main_kernel(dyn, ops, scale, cost, out):
    count = cost[...].astype(F32).astype(BF16)
    count2 = jnp.concatenate([count, count], axis=1)
    pairs = GROUP // 2

    def begin(base, p):
        return jnp.concatenate([dyn[base + 2 * p], dyn[base + 2 * p + 1]], axis=1)

    def group(g, carry):
        base = g * GROUP
        state = [begin(base, p) for p in range(pairs)]
        for s in range(KMAX):
            for p in range(pairs):
                both = dot(ops[s], state[p])
                tiles = []
                for t in range(LEVELS // TILE):
                    flat = both[2 * t * TILE : (2 * t + 1) * TILE]
                    bent = both[(2 * t + 1) * TILE : (2 * t + 2) * TILE]
                    factor = scale[t * TILE : (t + 1) * TILE]
                    factor = jnp.concatenate([factor, factor], axis=1)
                    tiles.append((flat + factor * bent).astype(BF16))
                widened = jnp.concatenate(tiles, axis=0)
                state[p] = widened if s == 0 else jnp.where(count2 > s, widened, state[p])
        for p in range(pairs):
            start = begin(base, p)
            result = start + (state[p] - start)
            for i in range(2):
                out[base + 2 * p + i] = result[:, i * COLS : (i + 1) * COLS]
        return carry

    lax.fori_loop(0, TRACERS // GROUP, group, 0)


def order_kernel(received, out):
    values = received[...]
    place = iota((COLS, COLS), 0)
    here = iota((COLS, COLS), 1)
    flags = values.astype(BF16)
    earlier = dot((here < place).astype(BF16), flags)
    first = values[:, TRACERS : TRACERS + 1]
    second = values[:, SLOT + TRACERS : SLOT + TRACERS + 1]
    rank = earlier[:, TRACERS : TRACERS + 1] + earlier[:, SLOT + TRACERS : SLOT + TRACERS + 1]
    spot = here.astype(F32)
    chosen = jnp.concatenate(
        [
            jnp.where(spot == rank, first, 0.0),
            jnp.where(spot == rank + first, second, 0.0),
        ],
        axis=0,
    ).astype(BF16)
    turned = values.T
    rows = jnp.concatenate([turned[:SLOT], turned[SLOT : 2 * SLOT]], axis=1)
    high, low = split(rows)
    out[...] = (dot(high, chosen) + dot(low, chosen))[:TRACERS]


def local(fields, neighbors, cost, dest, diffusivity, operators):
    size = lax.axis_size("narrow")
    up = [(i, (i + 1) % size) for i in range(size)]
    down = [(j, i) for i, j in up]
    flat = fields.reshape(TRACERS, LEVELS, COLS)
    vmem = pl.BlockSpec(memory_space=pltpu.VMEM)
    params = pltpu.CompilerParams(vmem_limit_bytes=ROOM)
    side = jax.ShapeDtypeStruct((REACH * TRACERS, LEVELS), BF16)
    left, right = pl.pallas_call(
        edge_kernel,
        out_shape=(side, side),
        in_specs=[vmem],
        out_specs=[vmem] * 2,
        scratch_shapes=[pltpu.VMEM((2 * REACH * TRACERS, LEVELS), F32)],
        compiler_params=params,
        name="edge",
    )(flat)
    before = lax.ppermute(right, "narrow", up)
    after = lax.ppermute(left, "narrow", down)
    square = jax.ShapeDtypeStruct((COLS, COLS), F32)
    ops, near, far, scale, pull, picked = pl.pallas_call(
        plan_kernel,
        out_shape=(
            jax.ShapeDtypeStruct((KMAX, 2 * LEVELS, LEVELS), BF16),
            jax.ShapeDtypeStruct((COLS, COLS), BF16),
            square,
            square,
            square,
            jax.ShapeDtypeStruct((COLS, 2 * COLS), BF16),
        ),
        in_specs=[vmem] * 5,
        out_specs=[vmem] * 6,
        scratch_shapes=[pltpu.VMEM((KMAX, 2 * LEVELS, LEVELS), BF16)],
        compiler_params=params,
        cost_estimate=pl.CostEstimate(flops=10**7, bytes_accessed=10**6, transcendentals=0),
        name="plan",
    )(
        *[
            pltpu.with_memory_space_constraint(x, pltpu.HBM)
            for x in (
                neighbors.reshape(NEIGH, COLS), cost, dest,
                diffusivity.reshape(LEVELS, COLS), operators,
            )
        ]
    )
    dyn, sent = pl.pallas_call(
        start_kernel,
        out_shape=(jax.ShapeDtypeStruct(flat.shape, BF16), square),
        in_specs=[vmem] * 7,
        out_specs=[vmem] * 2,
        scratch_shapes=[pltpu.VMEM((LEVELS, COLS), BF16), pltpu.VMEM((SLOT, COLS), F32)],
        compiler_params=params,
        name="start",
    )(flat, before, after, near, far, pull, picked)
    received = lax.all_to_all(sent, ("wide", "narrow"), split_axis=0, concat_axis=0, tiled=True)
    new = pl.pallas_call(
        main_kernel,
        out_shape=jax.ShapeDtypeStruct(flat.shape, BF16),
        in_specs=[vmem] * 4,
        out_specs=vmem,
        compiler_params=params,
        cost_estimate=pl.CostEstimate(flops=10**10, bytes_accessed=10**7, transcendentals=0),
        name="physics",
    )(dyn, ops, scale, cost)
    burden = pl.pallas_call(
        order_kernel,
        out_shape=jax.ShapeDtypeStruct((TRACERS, COLS), F32),
        in_specs=[vmem],
        out_specs=vmem,
        compiler_params=params,
        name="order",
    )(received)
    return new.reshape(fields.shape), burden[None]


def solution(mesh):
    in_specs = (
        P(None, None, "wide", "narrow"),
        P(None, "wide", "narrow"),
        P("wide", "narrow"),
        P("wide", "narrow"),
        P(None, "wide", "narrow"),
        P(),
    )
    out_specs = (P(None, None, "wide", "narrow"), P(("wide", "narrow"), None, None))
    return jax.shard_map(local, mesh=mesh, in_specs=in_specs, out_specs=out_specs, check_vma=False)
```

```python
import functools

import jax
import jax.numpy as jnp
from jax import lax
from jax.experimental import pallas as pl
from jax.experimental.pallas import tpu as pltpu
from jax.sharding import PartitionSpec as P

REACH = 2
NEIGH = 4
KMAX = 8
MIX = 0.2
TRACERS = 24
LEVELS = 128
COLS = 128
GROUP = 12
SLOT = 32
TILE = 16
TURNS = TILE // REACH
SIDE = REACH * TRACERS
NEAR = 8
CHAINS = 2
ROOM = 24 << 20

F32 = jnp.float32
BF16 = jnp.bfloat16
NT = (((1,), (1,)), ((), ()))


def iota(shape, dim):
    return lax.broadcasted_iota(jnp.int32, shape, dim)


def dot(a, b):
    return jnp.dot(a, b, preferred_element_type=F32)


def split(x):
    high = x.astype(BF16)
    return high, (x - high.astype(F32)).astype(BF16)


def level_laplace(z):
    above = jnp.concatenate([z[:1], z[:-1]], axis=0)
    below = jnp.concatenate([z[1:], z[-1:]], axis=0)
    return above + below - 2.0 * z


def edge_kernel(fields, left, right, own, left_rows, right_rows, own_rows):
    place = iota((NEAR, COLS), 0)
    lane = iota((NEAR, COLS), 1)
    edge = jnp.where(place < NEAR // 2, place, place + (COLS - NEAR))
    pick = (lane == edge).astype(BF16)
    for q in range(TRACERS):
        got = lax.dot_general(pick, fields[q], NT, preferred_element_type=F32)
        own_rows[NEAR * q : NEAR * (q + 1)] = got
        left_rows[REACH * q : REACH * (q + 1)] = got[:REACH]
        right_rows[REACH * q : REACH * (q + 1)] = got[NEAR - REACH :]
    left[...] = left_rows[...].astype(BF16)
    right[...] = right_rows[...].astype(BF16)
    own[: NEAR * TRACERS] = own_rows[...].astype(BF16)
    own[NEAR * TRACERS :] = jnp.zeros((2 * COLS - NEAR * TRACERS, LEVELS), BF16)


def halo_rows(before, after):
    gap = jnp.zeros((COLS // 2 - SIDE, LEVELS), BF16)
    return jnp.concatenate([before[...], gap, after[...], gap], axis=0)


def slots(values, axis):
    none = jnp.zeros(values.shape, values.dtype)
    first = jnp.concatenate([values, none], axis=axis)
    second = jnp.concatenate([none, values], axis=axis)
    return first, second


def plan_kernel(
    fields, own, meta, coef, operators,
    ops, near, far, scale, picked_edge, reach_edge, pull_edge, base_edge, count, base,
    pair, start, burden,
):
    for s in reversed(range(KMAX)):
        op = operators[s]
        lap = level_laplace(op.astype(F32)).astype(BF16)
        pair[s, :LEVELS] = op
        pair[s, LEVELS:] = lap
        for t in range(LEVELS // TILE):
            ops[s, 2 * t * TILE : (2 * t + 1) * TILE] = op[t * TILE : (t + 1) * TILE]
            ops[s, (2 * t + 1) * TILE : (2 * t + 2) * TILE] = lap[t * TILE : (t + 1) * TILE]

    steps = meta[NEIGH : NEIGH + 1, :].astype(F32)
    count[...] = steps
    steps = jnp.broadcast_to(steps, (COLS, COLS))
    scaled = coef[...].astype(F32) * (steps / (4.0 * KMAX))
    scale[...] = scaled
    scaled = scaled.T
    steps = steps.T

    place = iota((COLS, COLS), 0)
    here = iota((COLS, COLS), 1)
    lane = iota((1, COLS), 1)
    half = COLS // 2
    outer = jnp.where(place < half, place % REACH - REACH, place % REACH + COLS)
    inner = jnp.where(place < half, place % REACH, place % REACH + (COLS - REACH))
    weight = (place == here).astype(F32)
    reach = jnp.zeros((COLS, COLS), F32)
    row16 = iota((TILE, COLS), 0)
    turn16 = row16 % REACH
    before = jnp.zeros((TILE, COLS), F32)
    after = jnp.zeros((TILE, COLS), F32)
    for k in range(NEIGH):
        offset = ((meta[k : k + 1, :] - lane + REACH) & (COLS - 1)) - REACH
        reads = lane + offset
        weight += (place == reads).astype(F32)
        reach += (outer == reads).astype(F32)
        before += (turn16 - REACH == reads).astype(F32)
        after += (turn16 + COLS == reads).astype(F32)
    near[...] = weight.astype(BF16)
    for v in range(TURNS):
        mine = row16 // REACH == v
        far[0, v] = jnp.where(mine, before, 0.0).astype(BF16)
        far[1, v] = jnp.where(mine, after, 0.0).astype(BF16)

    target = jnp.broadcast_to(meta[NEIGH + 1 : NEIGH + 2, :], (COLS, COLS)).astype(F32)
    same = (target.T == target) & (place < here)
    turn = jnp.sum(same.astype(F32), axis=0, keepdims=True)
    to = (target == place.astype(F32)).astype(F32)
    picked = jnp.concatenate(
        [(to * (turn == 0.0)).astype(BF16), (to * (turn == 1.0)).astype(BF16)], axis=1
    )

    chosen = (inner == here).astype(BF16)
    for i in range(2):
        cols = slice(i * COLS, (i + 1) * COLS)
        picked_edge[:, cols] = lax.dot_general(
            picked[:, cols], chosen, NT, preferred_element_type=F32
        ).astype(BF16)
    tracer = (place % half) // REACH
    got = lax.dot_general(chosen, reach.astype(BF16), NT, preferred_element_type=F32)
    reach_edge[...] = jnp.where(tracer == (here % half) // REACH, got, 0.0).astype(BF16)
    got = lax.dot_general(chosen, near[...], NT, preferred_element_type=F32).astype(BF16)
    wide = (COLS, 2 * COLS)
    col = iota(wide, 1) % NEAR
    col = jnp.where(col < NEAR // 2, col, col + (COLS - NEAR))
    got = dot(got, (iota(wide, 0) == col).astype(BF16))
    mine = (iota(wide, 0) % half) // REACH == iota(wide, 1) // NEAR
    base_edge[...] = dot(jnp.where(mine, got, 0.0).astype(BF16), own[...])

    part = COLS // CHAINS
    held = [slice(i * part, (i + 1) * part) for i in range(CHAINS)]
    state = [jnp.ones((part, LEVELS), F32)] * CHAINS
    for s in reversed(range(KMAX)):
        for i, cols in enumerate(held):
            parts = []
            for pieces in zip(split(state[i]), split(scaled[cols] * state[i])):
                parts.append(jnp.concatenate(pieces, axis=1))
            moved = dot(jnp.concatenate(parts, axis=0), pair[s])
            state[i] = jnp.where(steps[cols] > s, moved[:part] + moved[part:], 1.0)
        for q in range((KMAX - 1 - s) * TRACERS // KMAX, (KMAX - s) * TRACERS // KMAX):
            start[q] = (MIX * dot(fields[q], near[...])).astype(BF16)
    pull = jnp.concatenate(state, axis=0) - 1.0
    high, low = split(pull)
    pull_edge[...] = dot(chosen, high) + dot(chosen, low)
    pull = pull.T

    for q in range(TRACERS):
        burden[q : q + 1, :] = jnp.sum(pull * start[q].astype(F32), axis=0, keepdims=True)
    inside = (lane >= REACH) & (lane < COLS - REACH)
    values = jnp.where(inside, burden[...], 0.0)
    flags = (iota((SLOT - TRACERS, COLS), 0) == 0).astype(F32)
    total = jnp.zeros((COLS, COLS), F32)
    for part in split(jnp.concatenate([values, flags], axis=0)):
        rows = [*slots(part, 1), jnp.zeros((2 * SLOT, 2 * COLS), BF16)]
        total += lax.dot_general(
            picked, jnp.concatenate(rows, axis=0), NT, preferred_element_type=F32
        )
    base[...] = total


def start_kernel(before, after, picked_edge, reach_edge, pull_edge, base_edge, base, sent):
    summed = base_edge[...] + dot(reach_edge[...], halo_rows(before, after))
    start = (MIX * summed).astype(BF16).astype(F32)
    values = jnp.sum(pull_edge[...] * start, axis=1, keepdims=True)
    tracer = (iota((COLS, COLS), 0) % (COLS // 2)) // REACH
    lane = iota((COLS, COLS), 1)
    total = base[...]
    for part in split(values):
        part = part.astype(F32)
        rows = [jnp.where(lane == tracer + i * SLOT, part, 0.0).astype(BF16) for i in range(2)]
        total += dot(picked_edge[...], jnp.concatenate(rows, axis=0))
    sent[...] = total


def main_kernel(fields, before, after, near, far, ops, scale, count, out, halo, dyn):
    halo[...] = halo_rows(before, after).astype(F32).T.astype(BF16)
    empty = jnp.zeros((TILE, COLS), BF16)
    for q in range(TRACERS):
        tiles = [empty] * (COLS // TILE)
        tiles[q // TURNS] = far[0, q % TURNS]
        tiles[COLS // TILE // 2 + q // TURNS] = far[1, q % TURNS]
        both = jnp.concatenate([fields[q], halo[...]], axis=1)
        summed = dot(both, jnp.concatenate([near[...], *tiles], axis=0))
        dyn[q] = (MIX * summed).astype(BF16)

    count2 = jnp.concatenate([count[...], count[...]], axis=1).astype(BF16)
    pairs = GROUP // 2

    def begin(base, p):
        return jnp.concatenate([dyn[base + 2 * p], dyn[base + 2 * p + 1]], axis=1)

    def group(g, carry):
        base = g * GROUP
        state = [begin(base, p) for p in range(pairs)]
        for s in range(KMAX):
            for p in range(pairs):
                both = dot(ops[s], state[p])
                tiles = []
                for t in range(LEVELS // TILE):
                    flat = both[2 * t * TILE : (2 * t + 1) * TILE]
                    bent = both[(2 * t + 1) * TILE : (2 * t + 2) * TILE]
                    factor = scale[t * TILE : (t + 1) * TILE]
                    factor = jnp.concatenate([factor, factor], axis=1)
                    tiles.append((flat + factor * bent).astype(BF16))
                widened = jnp.concatenate(tiles, axis=0)
                state[p] = widened if s == 0 else jnp.where(count2 > s, widened, state[p])
        for p in range(pairs):
            start = begin(base, p)
            result = start + (state[p] - start)
            for i in range(2):
                out[base + 2 * p + i] = result[:, i * COLS : (i + 1) * COLS]
        return carry

    lax.fori_loop(0, TRACERS // GROUP, group, 0)


def order_kernel(received, out):
    values = received[...]
    place = iota((COLS, COLS), 0)
    here = iota((COLS, COLS), 1)
    flags = values.astype(BF16)
    earlier = dot((here < place).astype(BF16), flags)
    first = values[:, TRACERS : TRACERS + 1]
    second = values[:, SLOT + TRACERS : SLOT + TRACERS + 1]
    rank = earlier[:, TRACERS : TRACERS + 1] + earlier[:, SLOT + TRACERS : SLOT + TRACERS + 1]
    spot = here.astype(F32)
    chosen = jnp.concatenate(
        [
            jnp.where(spot == rank, first, 0.0),
            jnp.where(spot == rank + first, second, 0.0),
        ],
        axis=0,
    ).astype(BF16)
    turned = values.T
    rows = jnp.concatenate([turned[:SLOT], turned[SLOT : 2 * SLOT]], axis=1)
    high, low = split(rows)
    out[...] = (dot(high, chosen) + dot(low, chosen))[:TRACERS]


def local(fields, neighbors, cost, dest, diffusivity, operators):
    size = lax.axis_size("narrow")
    up = [(i, (i + 1) % size) for i in range(size)]
    down = [(j, i) for i, j in up]
    flat = fields.reshape(TRACERS, LEVELS, COLS)
    vmem = pl.BlockSpec(memory_space=pltpu.VMEM)
    params = pltpu.CompilerParams(vmem_limit_bytes=ROOM)
    side = jax.ShapeDtypeStruct((SIDE, LEVELS), BF16)
    vmem = pl.BlockSpec(memory_space=pltpu.VMEM)
    params = pltpu.CompilerParams(vmem_limit_bytes=ROOM)
    meta = jnp.concatenate([neighbors.reshape(NEIGH, COLS), cost, dest, cost, dest], axis=0)
    left, right, own = pl.pallas_call(
        edge_kernel,
        out_shape=(side, side, jax.ShapeDtypeStruct((2 * COLS, LEVELS), BF16)),
        in_specs=[vmem],
        out_specs=[vmem] * 3,
        scratch_shapes=[
            pltpu.VMEM((SIDE, LEVELS), F32),
            pltpu.VMEM((SIDE, LEVELS), F32),
            pltpu.VMEM((NEAR * TRACERS, LEVELS), F32),
        ],
        compiler_params=params,
        cost_estimate=pl.CostEstimate(flops=2 * 10**9, bytes_accessed=4 * 10**6, transcendentals=0),
        name="edge",
    )(flat)
    before = lax.ppermute(right, "narrow", up)
    after = lax.ppermute(left, "narrow", down)
    square = jax.ShapeDtypeStruct((COLS, COLS), F32)
    square16 = jax.ShapeDtypeStruct((COLS, COLS), BF16)
    ops, near, far, scale, picked_edge, reach_edge, pull_edge, base_edge, count, base = pl.pallas_call(
        plan_kernel,
        out_shape=(
            jax.ShapeDtypeStruct((KMAX, 2 * LEVELS, LEVELS), BF16),
            square16,
            jax.ShapeDtypeStruct((2, TURNS, TILE, COLS), BF16),
            square,
            jax.ShapeDtypeStruct((COLS, 2 * COLS), BF16),
            square16,
            square,
            square,
            jax.ShapeDtypeStruct((1, COLS), F32),
            square,
        ),
        in_specs=[vmem] * 5,
        out_specs=[vmem] * 10,
        scratch_shapes=[
            pltpu.VMEM((KMAX, 2 * LEVELS, LEVELS), BF16),
            pltpu.VMEM((TRACERS, LEVELS, COLS), BF16),
            pltpu.VMEM((TRACERS, COLS), F32),
        ],
        compiler_params=params,
        cost_estimate=pl.CostEstimate(flops=10**7, bytes_accessed=10**6, transcendentals=0),
        name="plan",
    )(flat, own, meta, diffusivity.reshape(LEVELS, COLS), operators)
    sent = pl.pallas_call(
        start_kernel,
        out_shape=square,
        in_specs=[vmem] * 7,
        out_specs=vmem,
        compiler_params=params,
        name="start",
    )(before, after, picked_edge, reach_edge, pull_edge, base_edge, base)
    received = lax.all_to_all(sent, ("wide", "narrow"), split_axis=0, concat_axis=0, tiled=True)
    new = pl.pallas_call(
        main_kernel,
        out_shape=jax.ShapeDtypeStruct(flat.shape, BF16),
        in_specs=[vmem] * 8,
        out_specs=vmem,
        scratch_shapes=[
            pltpu.VMEM((LEVELS, COLS), BF16),
            pltpu.VMEM((TRACERS, LEVELS, COLS), BF16),
        ],
        compiler_params=params,
        cost_estimate=pl.CostEstimate(flops=10**10, bytes_accessed=10**7, transcendentals=0),
        name="physics",
    )(flat, before, after, near, far, ops, scale, count)
    burden = pl.pallas_call(
        order_kernel,
        out_shape=jax.ShapeDtypeStruct((TRACERS, COLS), F32),
        in_specs=[vmem],
        out_specs=vmem,
        compiler_params=params,
        name="order",
    )(received)
    return new.reshape(fields.shape), burden[None]


def solution(mesh):
    in_specs = (
        P(None, None, "wide", "narrow"),
        P(None, "wide", "narrow"),
        P("wide", "narrow"),
        P("wide", "narrow"),
        P(None, "wide", "narrow"),
        P(),
    )
    out_specs = (P(None, None, "wide", "narrow"), P(("wide", "narrow"), None, None))
    return jax.shard_map(local, mesh=mesh, in_specs=in_specs, out_specs=out_specs, check_vma=False)
```

```python
import functools

import jax
import jax.numpy as jnp
from jax import lax
from jax.experimental import pallas as pl
from jax.experimental.pallas import tpu as pltpu
from jax.sharding import PartitionSpec as P

REACH = 2
NEIGH = 4
KMAX = 8
MIX = 0.2
TRACERS = 24
LEVELS = 128
COLS = 128
GROUP = 12
SLOT = 32
TILE = 16
TURNS = TILE // REACH
SIDE = REACH * TRACERS
NEAR = 8
CHAINS = 2
ROOM = 24 << 20

F32 = jnp.float32
BF16 = jnp.bfloat16
NT = (((1,), (1,)), ((), ()))


def iota(shape, dim):
    return lax.broadcasted_iota(jnp.int32, shape, dim)


def dot(a, b):
    return jnp.dot(a, b, preferred_element_type=F32)


def split(x):
    high = x.astype(BF16)
    return high, (x - high.astype(F32)).astype(BF16)


def level_laplace(z):
    above = jnp.concatenate([z[:1], z[:-1]], axis=0)
    below = jnp.concatenate([z[1:], z[-1:]], axis=0)
    return above + below - 2.0 * z


def edge_kernel(fields, left, right, own, left_rows, right_rows, own_rows):
    place = iota((NEAR, COLS), 0)
    lane = iota((NEAR, COLS), 1)
    edge = jnp.where(place < NEAR // 2, place, place + (COLS - NEAR))
    pick = (lane == edge).astype(BF16)
    for q in range(TRACERS):
        got = lax.dot_general(pick, fields[q], NT, preferred_element_type=F32)
        own_rows[NEAR * q : NEAR * (q + 1)] = got
        left_rows[REACH * q : REACH * (q + 1)] = got[:REACH]
        right_rows[REACH * q : REACH * (q + 1)] = got[NEAR - REACH :]
    left[...] = left_rows[...].astype(BF16)
    right[...] = right_rows[...].astype(BF16)
    own[: NEAR * TRACERS] = own_rows[...].astype(BF16)
    own[NEAR * TRACERS :] = jnp.zeros((2 * COLS - NEAR * TRACERS, LEVELS), BF16)


def halo_rows(before, after):
    gap = jnp.zeros((COLS // 2 - SIDE, LEVELS), BF16)
    return jnp.concatenate([before[...], gap, after[...], gap], axis=0)


def slots(values, axis):
    none = jnp.zeros(values.shape, values.dtype)
    first = jnp.concatenate([values, none], axis=axis)
    second = jnp.concatenate([none, values], axis=axis)
    return first, second


def plan_kernel(
    fields, own, meta, coef, operators,
    ops, near, far, scale, picked_edge, reach_edge, pull_edge, base_edge, count, base,
    pair, start, burden,
):
    for s in reversed(range(KMAX)):
        op = operators[s]
        lap = level_laplace(op.astype(F32)).astype(BF16)
        pair[s, :LEVELS] = op
        pair[s, LEVELS:] = lap
        for t in range(LEVELS // TILE):
            ops[s, 2 * t * TILE : (2 * t + 1) * TILE] = op[t * TILE : (t + 1) * TILE]
            ops[s, (2 * t + 1) * TILE : (2 * t + 2) * TILE] = lap[t * TILE : (t + 1) * TILE]

    steps = meta[NEIGH : NEIGH + 1, :].astype(F32)
    count[...] = steps
    steps = jnp.broadcast_to(steps, (COLS, COLS))
    scaled = coef[...].astype(F32) * (steps / (4.0 * KMAX))
    scale[...] = scaled
    scaled = scaled.T
    steps = steps.T

    place = iota((COLS, COLS), 0)
    here = iota((COLS, COLS), 1)
    lane = iota((1, COLS), 1)
    half = COLS // 2
    outer = jnp.where(place < half, place % REACH - REACH, place % REACH + COLS)
    inner = jnp.where(place < half, place % REACH, place % REACH + (COLS - REACH))
    weight = (place == here).astype(F32)
    reach = jnp.zeros((COLS, COLS), F32)
    row16 = iota((TILE, COLS), 0)
    turn16 = row16 % REACH
    before = jnp.zeros((TILE, COLS), F32)
    after = jnp.zeros((TILE, COLS), F32)
    for k in range(NEIGH):
        offset = ((meta[k : k + 1, :] - lane + REACH) & (COLS - 1)) - REACH
        reads = lane + offset
        weight += (place == reads).astype(F32)
        reach += (outer == reads).astype(F32)
        before += (turn16 - REACH == reads).astype(F32)
        after += (turn16 + COLS == reads).astype(F32)
    near[...] = weight.astype(BF16)
    for v in range(TURNS):
        mine = row16 // REACH == v
        far[0, v] = jnp.where(mine, before, 0.0).astype(BF16)
        far[1, v] = jnp.where(mine, after, 0.0).astype(BF16)

    target = jnp.broadcast_to(meta[NEIGH + 1 : NEIGH + 2, :], (COLS, COLS)).astype(F32)
    same = (target.T == target) & (place < here)
    turn = jnp.sum(same.astype(F32), axis=0, keepdims=True)
    to = (target == place.astype(F32)).astype(F32)
    picked = jnp.concatenate(
        [(to * (turn == 0.0)).astype(BF16), (to * (turn == 1.0)).astype(BF16)], axis=1
    )

    chosen = (inner == here).astype(BF16)
    for i in range(2):
        cols = slice(i * COLS, (i + 1) * COLS)
        picked_edge[:, cols] = lax.dot_general(
            picked[:, cols], chosen, NT, preferred_element_type=F32
        ).astype(BF16)
    tracer = (place % half) // REACH
    got = lax.dot_general(chosen, reach.astype(BF16), NT, preferred_element_type=F32)
    reach_edge[...] = jnp.where(tracer == (here % half) // REACH, got, 0.0).astype(BF16)
    got = lax.dot_general(chosen, near[...], NT, preferred_element_type=F32).astype(BF16)
    wide = (COLS, 2 * COLS)
    col = iota(wide, 1) % NEAR
    col = jnp.where(col < NEAR // 2, col, col + (COLS - NEAR))
    got = dot(got, (iota(wide, 0) == col).astype(BF16))
    mine = (iota(wide, 0) % half) // REACH == iota(wide, 1) // NEAR
    base_edge[...] = dot(jnp.where(mine, got, 0.0).astype(BF16), own[...])

    part = COLS // CHAINS
    held = [slice(i * part, (i + 1) * part) for i in range(CHAINS)]
    state = [jnp.ones((part, LEVELS), F32)] * CHAINS
    for s in reversed(range(KMAX)):
        for i, cols in enumerate(held):
            parts = []
            for pieces in zip(split(state[i]), split(scaled[cols] * state[i])):
                parts.append(jnp.concatenate(pieces, axis=1))
            moved = dot(jnp.concatenate(parts, axis=0), pair[s])
            state[i] = jnp.where(steps[cols] > s, moved[:part] + moved[part:], 1.0)
        for q in range((KMAX - 1 - s) * TRACERS // KMAX, (KMAX - s) * TRACERS // KMAX):
            start[q] = (MIX * dot(fields[q], near[...])).astype(BF16)
    pull = jnp.concatenate(state, axis=0) - 1.0
    high, low = split(pull)
    pull_edge[...] = dot(chosen, high) + dot(chosen, low)
    pull = pull.T

    for q in range(TRACERS):
        burden[q : q + 1, :] = jnp.sum(pull * start[q].astype(F32), axis=0, keepdims=True)
    inside = (lane >= REACH) & (lane < COLS - REACH)
    values = jnp.where(inside, burden[...], 0.0)
    flags = (iota((SLOT - TRACERS, COLS), 0) == 0).astype(F32)
    total = jnp.zeros((COLS, COLS), F32)
    for part in split(jnp.concatenate([values, flags], axis=0)):
        rows = [*slots(part, 1), jnp.zeros((2 * SLOT, 2 * COLS), BF16)]
        total += lax.dot_general(
            picked, jnp.concatenate(rows, axis=0), NT, preferred_element_type=F32
        )
    base[...] = total


def start_kernel(before, after, picked_edge, reach_edge, pull_edge, base_edge, base, sent):
    summed = base_edge[...] + dot(reach_edge[...], halo_rows(before, after))
    start = (MIX * summed).astype(BF16).astype(F32)
    values = jnp.sum(pull_edge[...] * start, axis=1, keepdims=True)
    tracer = (iota((COLS, COLS), 0) % (COLS // 2)) // REACH
    lane = iota((COLS, COLS), 1)
    total = base[...]
    for part in split(values):
        part = part.astype(F32)
        rows = [jnp.where(lane == tracer + i * SLOT, part, 0.0).astype(BF16) for i in range(2)]
        total += dot(picked_edge[...], jnp.concatenate(rows, axis=0))
    sent[...] = total


def main_kernel(fields, before, after, near, far, ops, scale, count, out, halo, dyn):
    halo[...] = halo_rows(before, after).astype(F32).T.astype(BF16)
    empty = jnp.zeros((TILE, COLS), BF16)
    for q in range(TRACERS):
        tiles = [empty] * (COLS // TILE)
        tiles[q // TURNS] = far[0, q % TURNS]
        tiles[COLS // TILE // 2 + q // TURNS] = far[1, q % TURNS]
        both = jnp.concatenate([fields[q], halo[...]], axis=1)
        summed = dot(both, jnp.concatenate([near[...], *tiles], axis=0))
        dyn[q] = (MIX * summed).astype(BF16)

    count2 = jnp.concatenate([count[...], count[...]], axis=1)
    pairs = GROUP // 2

    def begin(base, p):
        return jnp.concatenate([dyn[base + 2 * p], dyn[base + 2 * p + 1]], axis=1)

    def group(g, carry):
        base = g * GROUP
        state = [begin(base, p) for p in range(pairs)]
        final = [None] * pairs
        for s in range(KMAX):
            for p in range(pairs):
                both = dot(ops[s], state[p])
                tiles, lasts = [], []
                for t in range(LEVELS // TILE):
                    flat = both[2 * t * TILE : (2 * t + 1) * TILE]
                    bent = both[(2 * t + 1) * TILE : (2 * t + 2) * TILE]
                    factor = scale[t * TILE : (t + 1) * TILE]
                    factor = jnp.concatenate([factor, factor], axis=1)
                    widened = flat + factor * bent
                    tiles.append(widened.astype(BF16))
                    lasts.append(widened if s == 0 else jnp.where(count2 > s, widened, final[p][t]))
                state[p], final[p] = jnp.concatenate(tiles, axis=0), lasts
        for p in range(pairs):
            start = begin(base, p).astype(F32)
            tend = (jnp.concatenate(final[p], axis=0) - start).astype(BF16)
            result = (start + tend.astype(F32)).astype(BF16)
            for i in range(2):
                out[base + 2 * p + i] = result[:, i * COLS : (i + 1) * COLS]
        return carry

    lax.fori_loop(0, TRACERS // GROUP, group, 0)


def order_kernel(received, out):
    values = received[...]
    place = iota((COLS, COLS), 0)
    here = iota((COLS, COLS), 1)
    flags = values.astype(BF16)
    earlier = dot((here < place).astype(BF16), flags)
    first = values[:, TRACERS : TRACERS + 1]
    second = values[:, SLOT + TRACERS : SLOT + TRACERS + 1]
    rank = earlier[:, TRACERS : TRACERS + 1] + earlier[:, SLOT + TRACERS : SLOT + TRACERS + 1]
    spot = here.astype(F32)
    chosen = jnp.concatenate(
        [
            jnp.where(spot == rank, first, 0.0),
            jnp.where(spot == rank + first, second, 0.0),
        ],
        axis=0,
    ).astype(BF16)
    turned = values.T
    rows = jnp.concatenate([turned[:SLOT], turned[SLOT : 2 * SLOT]], axis=1)
    high, low = split(rows)
    out[...] = (dot(high, chosen) + dot(low, chosen))[:TRACERS]


def local(fields, neighbors, cost, dest, diffusivity, operators):
    size = lax.axis_size("narrow")
    up = [(i, (i + 1) % size) for i in range(size)]
    down = [(j, i) for i, j in up]
    flat = fields.reshape(TRACERS, LEVELS, COLS)
    vmem = pl.BlockSpec(memory_space=pltpu.VMEM)
    params = pltpu.CompilerParams(vmem_limit_bytes=ROOM)
    side = jax.ShapeDtypeStruct((SIDE, LEVELS), BF16)
    vmem = pl.BlockSpec(memory_space=pltpu.VMEM)
    params = pltpu.CompilerParams(vmem_limit_bytes=ROOM)
    meta = jnp.concatenate([neighbors.reshape(NEIGH, COLS), cost, dest, cost, dest], axis=0)
    left, right, own = pl.pallas_call(
        edge_kernel,
        out_shape=(side, side, jax.ShapeDtypeStruct((2 * COLS, LEVELS), BF16)),
        in_specs=[vmem],
        out_specs=[vmem] * 3,
        scratch_shapes=[
            pltpu.VMEM((SIDE, LEVELS), F32),
            pltpu.VMEM((SIDE, LEVELS), F32),
            pltpu.VMEM((NEAR * TRACERS, LEVELS), F32),
        ],
        compiler_params=params,
        cost_estimate=pl.CostEstimate(flops=2 * 10**9, bytes_accessed=4 * 10**6, transcendentals=0),
        name="edge",
    )(flat)
    before = lax.ppermute(right, "narrow", up)
    after = lax.ppermute(left, "narrow", down)
    square = jax.ShapeDtypeStruct((COLS, COLS), F32)
    square16 = jax.ShapeDtypeStruct((COLS, COLS), BF16)
    ops, near, far, scale, picked_edge, reach_edge, pull_edge, base_edge, count, base = pl.pallas_call(
        plan_kernel,
        out_shape=(
            jax.ShapeDtypeStruct((KMAX, 2 * LEVELS, LEVELS), BF16),
            square16,
            jax.ShapeDtypeStruct((2, TURNS, TILE, COLS), BF16),
            square,
            jax.ShapeDtypeStruct((COLS, 2 * COLS), BF16),
            square16,
            square,
            square,
            jax.ShapeDtypeStruct((1, COLS), F32),
            square,
        ),
        in_specs=[vmem] * 5,
        out_specs=[vmem] * 10,
        scratch_shapes=[
            pltpu.VMEM((KMAX, 2 * LEVELS, LEVELS), BF16),
            pltpu.VMEM((TRACERS, LEVELS, COLS), BF16),
            pltpu.VMEM((TRACERS, COLS), F32),
        ],
        compiler_params=params,
        cost_estimate=pl.CostEstimate(flops=10**7, bytes_accessed=10**6, transcendentals=0),
        name="plan",
    )(flat, own, meta, diffusivity.reshape(LEVELS, COLS), operators)
    sent = pl.pallas_call(
        start_kernel,
        out_shape=square,
        in_specs=[vmem] * 7,
        out_specs=vmem,
        compiler_params=params,
        name="start",
    )(before, after, picked_edge, reach_edge, pull_edge, base_edge, base)
    received = lax.all_to_all(sent, ("wide", "narrow"), split_axis=0, concat_axis=0, tiled=True)
    new = pl.pallas_call(
        main_kernel,
        out_shape=jax.ShapeDtypeStruct(flat.shape, BF16),
        in_specs=[vmem] * 8,
        out_specs=vmem,
        scratch_shapes=[
            pltpu.VMEM((LEVELS, COLS), BF16),
            pltpu.VMEM((TRACERS, LEVELS, COLS), BF16),
        ],
        compiler_params=params,
        cost_estimate=pl.CostEstimate(flops=10**10, bytes_accessed=10**7, transcendentals=0),
        name="physics",
    )(flat, before, after, near, far, ops, scale, count)
    burden = pl.pallas_call(
        order_kernel,
        out_shape=jax.ShapeDtypeStruct((TRACERS, COLS), F32),
        in_specs=[vmem],
        out_specs=vmem,
        compiler_params=params,
        name="order",
    )(received)
    return new.reshape(fields.shape), burden[None]


def solution(mesh):
    in_specs = (
        P(None, None, "wide", "narrow"),
        P(None, "wide", "narrow"),
        P("wide", "narrow"),
        P("wide", "narrow"),
        P(None, "wide", "narrow"),
        P(),
    )
    out_specs = (P(None, None, "wide", "narrow"), P(("wide", "narrow"), None, None))
    return jax.shard_map(local, mesh=mesh, in_specs=in_specs, out_specs=out_specs, check_vma=False)
```

```python
import functools

import jax
import jax.numpy as jnp
from jax import lax
from jax.experimental import pallas as pl
from jax.experimental.pallas import tpu as pltpu
from jax.sharding import PartitionSpec as P

REACH = 2
NEIGH = 4
KMAX = 8
MIX = 0.2
TRACERS = 24
LEVELS = 128
COLS = 128
GROUP = 12
SLOT = 32
TILE = 16
TURNS = TILE // REACH
SIDE = REACH * TRACERS
NEAR = 8
CHAINS = 2
ROOM = 24 << 20

F32 = jnp.float32
BF16 = jnp.bfloat16
NT = (((1,), (1,)), ((), ()))


def iota(shape, dim):
    return lax.broadcasted_iota(jnp.int32, shape, dim)


def dot(a, b):
    return jnp.dot(a, b, preferred_element_type=F32)


def split(x):
    high = x.astype(BF16)
    return high, (x - high.astype(F32)).astype(BF16)


def level_laplace(z):
    above = jnp.concatenate([z[:1], z[:-1]], axis=0)
    below = jnp.concatenate([z[1:], z[-1:]], axis=0)
    return above + below - 2.0 * z


def edge_kernel(fields, left, right, own, left_rows, right_rows, own_rows):
    place = iota((NEAR, COLS), 0)
    lane = iota((NEAR, COLS), 1)
    edge = jnp.where(place < NEAR // 2, place, place + (COLS - NEAR))
    pick = (lane == edge).astype(BF16)
    for q in range(TRACERS):
        got = lax.dot_general(pick, fields[q], NT, preferred_element_type=F32)
        own_rows[NEAR * q : NEAR * (q + 1)] = got
        left_rows[REACH * q : REACH * (q + 1)] = got[:REACH]
        right_rows[REACH * q : REACH * (q + 1)] = got[NEAR - REACH :]
    left[...] = left_rows[...].astype(BF16)
    right[...] = right_rows[...].astype(BF16)
    own[: NEAR * TRACERS] = own_rows[...].astype(BF16)
    own[NEAR * TRACERS :] = jnp.zeros((2 * COLS - NEAR * TRACERS, LEVELS), BF16)


def halo_rows(before, after):
    gap = jnp.zeros((COLS // 2 - SIDE, LEVELS), BF16)
    return jnp.concatenate([before[...], gap, after[...], gap], axis=0)


def slots(values, axis):
    none = jnp.zeros(values.shape, values.dtype)
    first = jnp.concatenate([values, none], axis=axis)
    second = jnp.concatenate([none, values], axis=axis)
    return first, second


def plan_kernel(
    fields, own, meta, coef, operators,
    ops, near, far, scale, picked_edge, reach_edge, pull_edge, base_edge, count, base,
    pair, start, burden,
):
    for s in reversed(range(KMAX)):
        op = operators[s]
        lap = level_laplace(op.astype(F32)).astype(BF16)
        pair[s, :LEVELS] = op
        pair[s, LEVELS:] = lap
        for t in range(LEVELS // TILE):
            ops[s, 2 * t * TILE : (2 * t + 1) * TILE] = op[t * TILE : (t + 1) * TILE]
            ops[s, (2 * t + 1) * TILE : (2 * t + 2) * TILE] = lap[t * TILE : (t + 1) * TILE]

    steps = meta[NEIGH : NEIGH + 1, :].astype(F32)
    count[...] = steps
    steps = jnp.broadcast_to(steps, (COLS, COLS))
    scaled = coef[...].astype(F32) * (steps / (4.0 * KMAX))
    scale[...] = scaled
    scaled = scaled.T
    steps = steps.T

    place = iota((COLS, COLS), 0)
    here = iota((COLS, COLS), 1)
    lane = iota((1, COLS), 1)
    half = COLS // 2
    outer = jnp.where(place < half, place % REACH - REACH, place % REACH + COLS)
    inner = jnp.where(place < half, place % REACH, place % REACH + (COLS - REACH))
    weight = (place == here).astype(F32)
    reach = jnp.zeros((COLS, COLS), F32)
    row16 = iota((TILE, COLS), 0)
    turn16 = row16 % REACH
    before = jnp.zeros((TILE, COLS), F32)
    after = jnp.zeros((TILE, COLS), F32)
    for k in range(NEIGH):
        offset = ((meta[k : k + 1, :] - lane + REACH) & (COLS - 1)) - REACH
        reads = lane + offset
        weight += (place == reads).astype(F32)
        reach += (outer == reads).astype(F32)
        before += (turn16 - REACH == reads).astype(F32)
        after += (turn16 + COLS == reads).astype(F32)
    near[...] = weight.astype(BF16)
    for v in range(TURNS):
        mine = row16 // REACH == v
        far[0, v] = jnp.where(mine, before, 0.0).astype(BF16)
        far[1, v] = jnp.where(mine, after, 0.0).astype(BF16)

    target = jnp.broadcast_to(meta[NEIGH + 1 : NEIGH + 2, :], (COLS, COLS)).astype(F32)
    same = (target.T == target) & (place < here)
    turn = jnp.sum(same.astype(F32), axis=0, keepdims=True)
    to = (target == place.astype(F32)).astype(F32)
    picked = jnp.concatenate(
        [(to * (turn == 0.0)).astype(BF16), (to * (turn == 1.0)).astype(BF16)], axis=1
    )

    chosen = (inner == here).astype(BF16)
    for i in range(2):
        cols = slice(i * COLS, (i + 1) * COLS)
        picked_edge[:, cols] = lax.dot_general(
            picked[:, cols], chosen, NT, preferred_element_type=F32
        ).astype(BF16)
    tracer = (place % half) // REACH
    got = lax.dot_general(chosen, reach.astype(BF16), NT, preferred_element_type=F32)
    reach_edge[...] = jnp.where(tracer == (here % half) // REACH, got, 0.0).astype(BF16)
    got = lax.dot_general(chosen, near[...], NT, preferred_element_type=F32).astype(BF16)
    wide = (COLS, 2 * COLS)
    col = iota(wide, 1) % NEAR
    col = jnp.where(col < NEAR // 2, col, col + (COLS - NEAR))
    got = dot(got, (iota(wide, 0) == col).astype(BF16))
    mine = (iota(wide, 0) % half) // REACH == iota(wide, 1) // NEAR
    base_edge[...] = dot(jnp.where(mine, got, 0.0).astype(BF16), own[...])

    part = COLS // CHAINS
    held = [slice(i * part, (i + 1) * part) for i in range(CHAINS)]
    state = [jnp.ones((part, LEVELS), F32)] * CHAINS
    for s in reversed(range(KMAX)):
        for i, cols in enumerate(held):
            parts = []
            for pieces in zip(split(state[i]), split(scaled[cols] * state[i])):
                parts.append(jnp.concatenate(pieces, axis=1))
            moved = dot(jnp.concatenate(parts, axis=0), pair[s])
            state[i] = jnp.where(steps[cols] > s, moved[:part] + moved[part:], 1.0)
        for q in range((KMAX - 1 - s) * TRACERS // KMAX, (KMAX - s) * TRACERS // KMAX):
            start[q] = (MIX * dot(fields[q], near[...])).astype(BF16)
    pull = jnp.concatenate(state, axis=0) - 1.0
    high, low = split(pull)
    pull_edge[...] = dot(chosen, high) + dot(chosen, low)
    pull = pull.T

    for q in range(TRACERS):
        burden[q : q + 1, :] = jnp.sum(pull * start[q].astype(F32), axis=0, keepdims=True)
    inside = (lane >= REACH) & (lane < COLS - REACH)
    values = jnp.where(inside, burden[...], 0.0)
    flags = (iota((SLOT - TRACERS, COLS), 0) == 0).astype(F32)
    total = jnp.zeros((COLS, COLS), F32)
    for part in split(jnp.concatenate([values, flags], axis=0)):
        rows = [*slots(part, 1), jnp.zeros((2 * SLOT, 2 * COLS), BF16)]
        total += lax.dot_general(
            picked, jnp.concatenate(rows, axis=0), NT, preferred_element_type=F32
        )
    base[...] = total


def start_kernel(before, after, picked_edge, reach_edge, pull_edge, base_edge, base, sent):
    summed = base_edge[...] + dot(reach_edge[...], halo_rows(before, after))
    start = (MIX * summed).astype(BF16).astype(F32)
    values = jnp.sum(pull_edge[...] * start, axis=1, keepdims=True)
    tracer = (iota((COLS, COLS), 0) % (COLS // 2)) // REACH
    lane = iota((COLS, COLS), 1)
    total = base[...]
    for part in split(values):
        part = part.astype(F32)
        rows = [jnp.where(lane == tracer + i * SLOT, part, 0.0).astype(BF16) for i in range(2)]
        total += dot(picked_edge[...], jnp.concatenate(rows, axis=0))
    sent[...] = total


def main_kernel(fields, before, after, near, far, ops, scale, count, out, halo, dyn):
    halo[...] = halo_rows(before, after).astype(F32).T.astype(BF16)
    empty = jnp.zeros((TILE, COLS), BF16)
    for q in range(TRACERS):
        tiles = [empty] * (COLS // TILE)
        tiles[q // TURNS] = far[0, q % TURNS]
        tiles[COLS // TILE // 2 + q // TURNS] = far[1, q % TURNS]
        both = jnp.concatenate([fields[q], halo[...]], axis=1)
        summed = dot(both, jnp.concatenate([near[...], *tiles], axis=0))
        dyn[q] = (MIX * summed).astype(BF16)

    count2 = jnp.concatenate([count[...], count[...]], axis=1)
    pairs = GROUP // 2

    def begin(base, p):
        return jnp.concatenate([dyn[base + 2 * p], dyn[base + 2 * p + 1]], axis=1)

    def group(g, carry):
        base = g * GROUP
        state = [begin(base, p) for p in range(pairs)]
        final = [None] * pairs
        for s in range(KMAX):
            for p in range(pairs):
                both = dot(ops[s], state[p])
                tiles, lasts = [], []
                for t in range(LEVELS // TILE):
                    flat = both[2 * t * TILE : (2 * t + 1) * TILE]
                    bent = both[(2 * t + 1) * TILE : (2 * t + 2) * TILE]
                    factor = scale[t * TILE : (t + 1) * TILE]
                    factor = jnp.concatenate([factor, factor], axis=1)
                    widened = flat + factor * bent
                    tiles.append(widened.astype(BF16))
                    lasts.append(widened if s == 0 else jnp.where(count2 > s, widened, final[p][t]))
                state[p], final[p] = jnp.concatenate(tiles, axis=0), lasts
        for p in range(pairs):
            start = begin(base, p).astype(F32)
            tend = (jnp.concatenate(final[p], axis=0) - start).astype(BF16)
            result = (start + tend.astype(F32)).astype(BF16)
            for i in range(2):
                out[base + 2 * p + i] = result[:, i * COLS : (i + 1) * COLS]
        return carry

    lax.fori_loop(0, TRACERS // GROUP, group, 0)


def order_kernel(received, out):
    values = received[...]
    place = iota((COLS, COLS), 0)
    here = iota((COLS, COLS), 1)
    flags = values.astype(BF16)
    earlier = dot((here < place).astype(BF16), flags)
    first = values[:, TRACERS : TRACERS + 1]
    second = values[:, SLOT + TRACERS : SLOT + TRACERS + 1]
    rank = earlier[:, TRACERS : TRACERS + 1] + earlier[:, SLOT + TRACERS : SLOT + TRACERS + 1]
    spot = here.astype(F32)
    chosen = jnp.concatenate(
        [
            jnp.where(spot == rank, first, 0.0),
            jnp.where(spot == rank + first, second, 0.0),
        ],
        axis=0,
    ).astype(BF16)
    turned = values.T
    rows = jnp.concatenate([turned[:SLOT], turned[SLOT : 2 * SLOT]], axis=1)
    high, low = split(rows)
    out[...] = (dot(high, chosen) + dot(low, chosen))[:TRACERS]


def local(fields, neighbors, cost, dest, diffusivity, operators):
    size = lax.axis_size("narrow")
    odd = lax.axis_index("narrow") % 2 == 1
    trades = [[(i, (i + 1 if i % 2 == turn else i - 1) % size) for i in range(size)] for turn in (1, 0)]
    flat = fields.reshape(TRACERS, LEVELS, COLS)
    vmem = pl.BlockSpec(memory_space=pltpu.VMEM)
    params = pltpu.CompilerParams(vmem_limit_bytes=ROOM)
    side = jax.ShapeDtypeStruct((SIDE, LEVELS), BF16)
    vmem = pl.BlockSpec(memory_space=pltpu.VMEM)
    params = pltpu.CompilerParams(vmem_limit_bytes=ROOM)
    meta = jnp.concatenate([neighbors.reshape(NEIGH, COLS), cost, dest, cost, dest], axis=0)
    left, right, own = pl.pallas_call(
        edge_kernel,
        out_shape=(side, side, jax.ShapeDtypeStruct((2 * COLS, LEVELS), BF16)),
        in_specs=[vmem],
        out_specs=[vmem] * 3,
        scratch_shapes=[
            pltpu.VMEM((SIDE, LEVELS), F32),
            pltpu.VMEM((SIDE, LEVELS), F32),
            pltpu.VMEM((NEAR * TRACERS, LEVELS), F32),
        ],
        compiler_params=params,
        cost_estimate=pl.CostEstimate(flops=2 * 10**9, bytes_accessed=4 * 10**6, transcendentals=0),
        name="edge",
    )(flat)
    first = lax.ppermute(jnp.where(odd, right, left), "narrow", trades[0])
    second = lax.ppermute(jnp.where(odd, left, right), "narrow", trades[1])
    before = jnp.where(odd, second, first)
    after = jnp.where(odd, first, second)
    square = jax.ShapeDtypeStruct((COLS, COLS), F32)
    square16 = jax.ShapeDtypeStruct((COLS, COLS), BF16)
    ops, near, far, scale, picked_edge, reach_edge, pull_edge, base_edge, count, base = pl.pallas_call(
        plan_kernel,
        out_shape=(
            jax.ShapeDtypeStruct((KMAX, 2 * LEVELS, LEVELS), BF16),
            square16,
            jax.ShapeDtypeStruct((2, TURNS, TILE, COLS), BF16),
            square,
            jax.ShapeDtypeStruct((COLS, 2 * COLS), BF16),
            square16,
            square,
            square,
            jax.ShapeDtypeStruct((1, COLS), F32),
            square,
        ),
        in_specs=[vmem] * 5,
        out_specs=[vmem] * 10,
        scratch_shapes=[
            pltpu.VMEM((KMAX, 2 * LEVELS, LEVELS), BF16),
            pltpu.VMEM((TRACERS, LEVELS, COLS), BF16),
            pltpu.VMEM((TRACERS, COLS), F32),
        ],
        compiler_params=params,
        cost_estimate=pl.CostEstimate(flops=10**7, bytes_accessed=10**6, transcendentals=0),
        name="plan",
    )(flat, own, meta, diffusivity.reshape(LEVELS, COLS), operators)
    sent = pl.pallas_call(
        start_kernel,
        out_shape=square,
        in_specs=[vmem] * 7,
        out_specs=vmem,
        compiler_params=params,
        name="start",
    )(before, after, picked_edge, reach_edge, pull_edge, base_edge, base)
    received = lax.all_to_all(sent, ("wide", "narrow"), split_axis=0, concat_axis=0, tiled=True)
    new = pl.pallas_call(
        main_kernel,
        out_shape=jax.ShapeDtypeStruct(flat.shape, BF16),
        in_specs=[vmem] * 8,
        out_specs=vmem,
        scratch_shapes=[
            pltpu.VMEM((LEVELS, COLS), BF16),
            pltpu.VMEM((TRACERS, LEVELS, COLS), BF16),
        ],
        compiler_params=params,
        cost_estimate=pl.CostEstimate(flops=10**10, bytes_accessed=10**7, transcendentals=0),
        name="physics",
    )(flat, before, after, near, far, ops, scale, count)
    burden = pl.pallas_call(
        order_kernel,
        out_shape=jax.ShapeDtypeStruct((TRACERS, COLS), F32),
        in_specs=[vmem],
        out_specs=vmem,
        compiler_params=params,
        name="order",
    )(received)
    return new.reshape(fields.shape), burden[None]


def solution(mesh):
    in_specs = (
        P(None, None, "wide", "narrow"),
        P(None, "wide", "narrow"),
        P("wide", "narrow"),
        P("wide", "narrow"),
        P(None, "wide", "narrow"),
        P(),
    )
    out_specs = (P(None, None, "wide", "narrow"), P(("wide", "narrow"), None, None))
    return jax.shard_map(local, mesh=mesh, in_specs=in_specs, out_specs=out_specs, check_vma=False)
```

```python
import functools

import jax
import jax.numpy as jnp
from jax import lax
from jax.experimental import pallas as pl
from jax.experimental.pallas import tpu as pltpu
from jax.sharding import PartitionSpec as P

REACH = 2
NEIGH = 4
KMAX = 8
MIX = 0.2
TRACERS = 24
LEVELS = 128
COLS = 128
GROUP = 12
SLOT = 32
TILE = 16
TURNS = TILE // REACH
SIDE = REACH * TRACERS
NEAR = 8
CHAINS = 2
ROOM = 24 << 20

F32 = jnp.float32
BF16 = jnp.bfloat16
NT = (((1,), (1,)), ((), ()))


def iota(shape, dim):
    return lax.broadcasted_iota(jnp.int32, shape, dim)


def dot(a, b):
    return jnp.dot(a, b, preferred_element_type=F32)


def split(x):
    high = x.astype(BF16)
    return high, (x - high.astype(F32)).astype(BF16)


def level_laplace(z):
    above = jnp.concatenate([z[:1], z[:-1]], axis=0)
    below = jnp.concatenate([z[1:], z[-1:]], axis=0)
    return above + below - 2.0 * z


def edge_kernel(fields, left, right, own, left_rows, right_rows, own_rows):
    place = iota((NEAR, COLS), 0)
    lane = iota((NEAR, COLS), 1)
    edge = jnp.where(place < NEAR // 2, place, place + (COLS - NEAR))
    pick = (lane == edge).astype(BF16)
    for q in range(TRACERS):
        got = lax.dot_general(pick, fields[q], NT, preferred_element_type=F32)
        own_rows[NEAR * q : NEAR * (q + 1)] = got
        left_rows[REACH * q : REACH * (q + 1)] = got[:REACH]
        right_rows[REACH * q : REACH * (q + 1)] = got[NEAR - REACH :]
    left[...] = left_rows[...].astype(BF16)
    right[...] = right_rows[...].astype(BF16)
    own[: NEAR * TRACERS] = own_rows[...].astype(BF16)
    own[NEAR * TRACERS :] = jnp.zeros((2 * COLS - NEAR * TRACERS, LEVELS), BF16)


def halo_rows(before, after):
    gap = jnp.zeros((COLS // 2 - SIDE, LEVELS), BF16)
    return jnp.concatenate([before[...], gap, after[...], gap], axis=0)


def slots(values, axis):
    none = jnp.zeros(values.shape, values.dtype)
    first = jnp.concatenate([values, none], axis=axis)
    second = jnp.concatenate([none, values], axis=axis)
    return first, second


def plan_kernel(
    fields, own, meta, coef, operators,
    ops, near, far, scale, picked_edge, reach_edge, pull_edge, base_edge, count, base,
    pair, start, burden,
):
    for s in reversed(range(KMAX)):
        op = operators[s]
        lap = level_laplace(op.astype(F32)).astype(BF16)
        pair[s, :LEVELS] = op
        pair[s, LEVELS:] = lap
        for t in range(LEVELS // TILE):
            ops[s, 2 * t * TILE : (2 * t + 1) * TILE] = op[t * TILE : (t + 1) * TILE]
            ops[s, (2 * t + 1) * TILE : (2 * t + 2) * TILE] = lap[t * TILE : (t + 1) * TILE]

    steps = meta[NEIGH : NEIGH + 1, :].astype(F32)
    count[...] = steps
    steps = jnp.broadcast_to(steps, (COLS, COLS))
    scaled = coef[...].astype(F32) * (steps / (4.0 * KMAX))
    scale[...] = scaled
    scaled = scaled.T
    steps = steps.T

    place = iota((COLS, COLS), 0)
    here = iota((COLS, COLS), 1)
    lane = iota((1, COLS), 1)
    half = COLS // 2
    outer = jnp.where(place < half, place % REACH - REACH, place % REACH + COLS)
    inner = jnp.where(place < half, place % REACH, place % REACH + (COLS - REACH))
    weight = (place == here).astype(F32)
    reach = jnp.zeros((COLS, COLS), F32)
    row16 = iota((TILE, COLS), 0)
    turn16 = row16 % REACH
    before = jnp.zeros((TILE, COLS), F32)
    after = jnp.zeros((TILE, COLS), F32)
    for k in range(NEIGH):
        offset = ((meta[k : k + 1, :] - lane + REACH) & (COLS - 1)) - REACH
        reads = lane + offset
        weight += (place == reads).astype(F32)
        reach += (outer == reads).astype(F32)
        before += (turn16 - REACH == reads).astype(F32)
        after += (turn16 + COLS == reads).astype(F32)
    near[...] = weight.astype(BF16)
    for v in range(TURNS):
        mine = row16 // REACH == v
        far[0, v] = jnp.where(mine, before, 0.0).astype(BF16)
        far[1, v] = jnp.where(mine, after, 0.0).astype(BF16)

    target = jnp.broadcast_to(meta[NEIGH + 1 : NEIGH + 2, :], (COLS, COLS)).astype(F32)
    same = (target.T == target) & (place < here)
    turn = jnp.sum(same.astype(F32), axis=0, keepdims=True)
    to = (target == place.astype(F32)).astype(F32)
    picked = jnp.concatenate(
        [(to * (turn == 0.0)).astype(BF16), (to * (turn == 1.0)).astype(BF16)], axis=1
    )

    chosen = (inner == here).astype(BF16)
    for i in range(2):
        cols = slice(i * COLS, (i + 1) * COLS)
        picked_edge[:, cols] = lax.dot_general(
            picked[:, cols], chosen, NT, preferred_element_type=F32
        ).astype(BF16)
    tracer = (place % half) // REACH
    got = lax.dot_general(chosen, reach.astype(BF16), NT, preferred_element_type=F32)
    reach_edge[...] = jnp.where(tracer == (here % half) // REACH, got, 0.0).astype(BF16)
    got = lax.dot_general(chosen, near[...], NT, preferred_element_type=F32).astype(BF16)
    wide = (COLS, 2 * COLS)
    col = iota(wide, 1) % NEAR
    col = jnp.where(col < NEAR // 2, col, col + (COLS - NEAR))
    got = dot(got, (iota(wide, 0) == col).astype(BF16))
    mine = (iota(wide, 0) % half) // REACH == iota(wide, 1) // NEAR
    base_edge[...] = dot(jnp.where(mine, got, 0.0).astype(BF16), own[...])

    part = COLS // CHAINS
    held = [slice(i * part, (i + 1) * part) for i in range(CHAINS)]
    state = [jnp.ones((part, LEVELS), F32)] * CHAINS
    for s in reversed(range(KMAX)):
        for i, cols in enumerate(held):
            parts = []
            for pieces in zip(split(state[i]), split(scaled[cols] * state[i])):
                parts.append(jnp.concatenate(pieces, axis=1))
            moved = dot(jnp.concatenate(parts, axis=0), pair[s])
            state[i] = jnp.where(steps[cols] > s, moved[:part] + moved[part:], 1.0)
        for q in range((KMAX - 1 - s) * TRACERS // KMAX, (KMAX - s) * TRACERS // KMAX):
            start[q] = (MIX * dot(fields[q], near[...])).astype(BF16)
    pull = jnp.concatenate(state, axis=0) - 1.0
    high, low = split(pull)
    pull_edge[...] = dot(chosen, high) + dot(chosen, low)
    pull = pull.T

    for q in range(TRACERS):
        burden[q : q + 1, :] = jnp.sum(pull * start[q].astype(F32), axis=0, keepdims=True)
    inside = (lane >= REACH) & (lane < COLS - REACH)
    values = jnp.where(inside, burden[...], 0.0)
    flags = (iota((SLOT - TRACERS, COLS), 0) == 0).astype(F32)
    total = jnp.zeros((COLS, COLS), F32)
    for part in split(jnp.concatenate([values, flags], axis=0)):
        rows = [*slots(part, 1), jnp.zeros((2 * SLOT, 2 * COLS), BF16)]
        total += lax.dot_general(
            picked, jnp.concatenate(rows, axis=0), NT, preferred_element_type=F32
        )
    base[...] = total


def start_kernel(before, after, picked_edge, reach_edge, pull_edge, base_edge, base, sent):
    summed = base_edge[...] + dot(reach_edge[...], halo_rows(before, after))
    start = (MIX * summed).astype(BF16).astype(F32)
    values = jnp.sum(pull_edge[...] * start, axis=1, keepdims=True)
    tracer = (iota((COLS, COLS), 0) % (COLS // 2)) // REACH
    lane = iota((COLS, COLS), 1)
    parts = []
    for part in split(values):
        part = part.astype(F32)
        rows = [jnp.where(lane == tracer + i * SLOT, part, 0.0).astype(BF16) for i in range(2)]
        parts.append(jnp.concatenate(rows, axis=0))
    moved = dot(picked_edge[...], jnp.concatenate(parts, axis=1))
    sent[...] = base[...] + moved[:, :COLS] + moved[:, COLS:]


def main_kernel(fields, before, after, near, far, ops, scale, count, out, halo, dyn):
    halo[...] = halo_rows(before, after).astype(F32).T.astype(BF16)
    empty = jnp.zeros((TILE, COLS), BF16)
    for q in range(TRACERS):
        tiles = [empty] * (COLS // TILE)
        tiles[q // TURNS] = far[0, q % TURNS]
        tiles[COLS // TILE // 2 + q // TURNS] = far[1, q % TURNS]
        both = jnp.concatenate([fields[q], halo[...]], axis=1)
        summed = dot(both, jnp.concatenate([near[...], *tiles], axis=0))
        dyn[q] = (MIX * summed).astype(BF16)

    count2 = jnp.concatenate([count[...], count[...]], axis=1)
    pairs = GROUP // 2

    def begin(base, p):
        return jnp.concatenate([dyn[base + 2 * p], dyn[base + 2 * p + 1]], axis=1)

    def group(g, carry):
        base = g * GROUP
        state = [begin(base, p) for p in range(pairs)]
        final = [None] * pairs
        for s in range(KMAX):
            for p in range(pairs):
                both = dot(ops[s], state[p])
                tiles, lasts = [], []
                for t in range(LEVELS // TILE):
                    flat = both[2 * t * TILE : (2 * t + 1) * TILE]
                    bent = both[(2 * t + 1) * TILE : (2 * t + 2) * TILE]
                    factor = scale[t * TILE : (t + 1) * TILE]
                    factor = jnp.concatenate([factor, factor], axis=1)
                    widened = flat + factor * bent
                    tiles.append(widened.astype(BF16))
                    lasts.append(widened if s == 0 else jnp.where(count2 > s, widened, final[p][t]))
                state[p], final[p] = jnp.concatenate(tiles, axis=0), lasts
        for p in range(pairs):
            start = begin(base, p).astype(F32)
            tend = (jnp.concatenate(final[p], axis=0) - start).astype(BF16)
            result = (start + tend.astype(F32)).astype(BF16)
            for i in range(2):
                out[base + 2 * p + i] = result[:, i * COLS : (i + 1) * COLS]
        return carry

    lax.fori_loop(0, TRACERS // GROUP, group, 0)


def order_kernel(received, out):
    values = received[...]
    place = iota((COLS, COLS), 0)
    here = iota((COLS, COLS), 1)
    flags = values.astype(BF16)
    earlier = dot((here < place).astype(BF16), flags)
    first = values[:, TRACERS : TRACERS + 1]
    second = values[:, SLOT + TRACERS : SLOT + TRACERS + 1]
    rank = earlier[:, TRACERS : TRACERS + 1] + earlier[:, SLOT + TRACERS : SLOT + TRACERS + 1]
    spot = here.astype(F32)
    chosen = jnp.concatenate(
        [
            jnp.where(spot == rank, first, 0.0),
            jnp.where(spot == rank + first, second, 0.0),
        ],
        axis=0,
    ).astype(BF16)
    turned = values.T
    rows = jnp.concatenate([turned[:SLOT], turned[SLOT : 2 * SLOT]], axis=1)
    high, low = split(rows)
    moved = dot(jnp.concatenate([high, low], axis=0), chosen)
    out[...] = moved[:TRACERS] + moved[SLOT : SLOT + TRACERS]


def local(fields, neighbors, cost, dest, diffusivity, operators):
    size = lax.axis_size("narrow")
    up = [(i, (i + 1) % size) for i in range(size)]
    down = [(j, i) for i, j in up]
    flat = fields.reshape(TRACERS, LEVELS, COLS)
    vmem = pl.BlockSpec(memory_space=pltpu.VMEM)
    params = pltpu.CompilerParams(vmem_limit_bytes=ROOM)
    side = jax.ShapeDtypeStruct((SIDE, LEVELS), BF16)
    vmem = pl.BlockSpec(memory_space=pltpu.VMEM)
    params = pltpu.CompilerParams(vmem_limit_bytes=ROOM)
    meta = jnp.concatenate([neighbors.reshape(NEIGH, COLS), cost, dest, cost, dest], axis=0)
    left, right, own = pl.pallas_call(
        edge_kernel,
        out_shape=(side, side, jax.ShapeDtypeStruct((2 * COLS, LEVELS), BF16)),
        in_specs=[vmem],
        out_specs=[vmem] * 3,
        scratch_shapes=[
            pltpu.VMEM((SIDE, LEVELS), F32),
            pltpu.VMEM((SIDE, LEVELS), F32),
            pltpu.VMEM((NEAR * TRACERS, LEVELS), F32),
        ],
        compiler_params=params,
        cost_estimate=pl.CostEstimate(flops=2 * 10**9, bytes_accessed=4 * 10**6, transcendentals=0),
        name="edge",
    )(flat)
    before = lax.ppermute(right, "narrow", up)
    after = lax.ppermute(left, "narrow", down)
    square = jax.ShapeDtypeStruct((COLS, COLS), F32)
    square16 = jax.ShapeDtypeStruct((COLS, COLS), BF16)
    ops, near, far, scale, picked_edge, reach_edge, pull_edge, base_edge, count, base = pl.pallas_call(
        plan_kernel,
        out_shape=(
            jax.ShapeDtypeStruct((KMAX, 2 * LEVELS, LEVELS), BF16),
            square16,
            jax.ShapeDtypeStruct((2, TURNS, TILE, COLS), BF16),
            square,
            jax.ShapeDtypeStruct((COLS, 2 * COLS), BF16),
            square16,
            square,
            square,
            jax.ShapeDtypeStruct((1, COLS), F32),
            square,
        ),
        in_specs=[vmem] * 5,
        out_specs=[vmem] * 10,
        scratch_shapes=[
            pltpu.VMEM((KMAX, 2 * LEVELS, LEVELS), BF16),
            pltpu.VMEM((TRACERS, LEVELS, COLS), BF16),
            pltpu.VMEM((TRACERS, COLS), F32),
        ],
        compiler_params=params,
        cost_estimate=pl.CostEstimate(flops=10**7, bytes_accessed=10**6, transcendentals=0),
        name="plan",
    )(flat, own, meta, diffusivity.reshape(LEVELS, COLS), operators)
    sent = pl.pallas_call(
        start_kernel,
        out_shape=square,
        in_specs=[vmem] * 7,
        out_specs=vmem,
        compiler_params=params,
        name="start",
    )(before, after, picked_edge, reach_edge, pull_edge, base_edge, base)
    received = lax.all_to_all(sent, ("wide", "narrow"), split_axis=0, concat_axis=0, tiled=True)
    new = pl.pallas_call(
        main_kernel,
        out_shape=jax.ShapeDtypeStruct(flat.shape, BF16),
        in_specs=[vmem] * 8,
        out_specs=vmem,
        scratch_shapes=[
            pltpu.VMEM((LEVELS, COLS), BF16),
            pltpu.VMEM((TRACERS, LEVELS, COLS), BF16),
        ],
        compiler_params=params,
        cost_estimate=pl.CostEstimate(flops=10**10, bytes_accessed=10**7, transcendentals=0),
        name="physics",
    )(flat, before, after, near, far, ops, scale, count)
    burden = pl.pallas_call(
        order_kernel,
        out_shape=jax.ShapeDtypeStruct((TRACERS, COLS), F32),
        in_specs=[vmem],
        out_specs=vmem,
        compiler_params=params,
        name="order",
    )(received)
    return new.reshape(fields.shape), burden[None]


def solution(mesh):
    in_specs = (
        P(None, None, "wide", "narrow"),
        P(None, "wide", "narrow"),
        P("wide", "narrow"),
        P("wide", "narrow"),
        P(None, "wide", "narrow"),
        P(),
    )
    out_specs = (P(None, None, "wide", "narrow"), P(("wide", "narrow"), None, None))
    return jax.shard_map(local, mesh=mesh, in_specs=in_specs, out_specs=out_specs, check_vma=False)
```
